512 devices in a mesh: ctx: 32 (over z_hi, y, core), tp: 16 (over z_lo, x).
Axes of the slice: x: 4, y: 8, z: 8 (z_hi: 2, z_lo: 4; z = z_hi * 4 + z_lo), core: 2. Of those that a mesh axis runs over, the one named last changes fastest.
Arguments:
- enc_query: bfloat16 [5120, 6144], P(('ctx', 'tp')), may hold values from -40 to 40
- enc_key: bfloat16 [5120, 6144], P(('ctx', 'tp')), may hold values from -5 to 5
- enc_value: bfloat16 [5120, 6144], P(('ctx', 'tp')), may hold values from -6 to 6
- dec_query: bfloat16 [1024, 6144], P(('ctx', 'tp')), may hold values from -40 to 40
- cross_key: bfloat16 [5120, 6144], P(('ctx', 'tp')), may hold values from -5 to 5
- cross_value: bfloat16 [5120, 6144], P(('ctx', 'tp')), may hold values from -6 to 6
Outputs:
- enc_context: bfloat16 [5120, 6144], P('ctx', 'tp')
- dec_context: bfloat16 [1024, 6144], P('ctx', 'tp')
The draws below stay inside these ranges and needn't reach their ends.
All inputs are finite; a program needn't handle non-finite values.
Results may differ from the reference program's by a relative error of at most 0.004.
Values may be sent and summed in bfloat16 or wider, within the bound.
A program may use at most 64 MiB of HBM per device.

```python
import jax
import jax.numpy as jnp
from jax import lax

HEADS = 48
HEAD_DIM = 128
HD = 6144
S_ENC = 5120
T_DEC = 1024


def paired(base_key, query_count, key_count, columns):
    query_seed = jax.random.fold_in(base_key, 11)
    key_seed = jax.random.fold_in(base_key, 12)
    query_draw = jax.random.truncated_normal(query_seed, -4.0, 4.0, (query_count, columns), jnp.float32) * 2.5
    key_draw = jax.random.truncated_normal(key_seed, -4.0, 4.0, (key_count, columns), jnp.float32) * 1.2
    return (query_draw, key_draw)


def draw_enc_query(key, part):
    return paired(jax.random.fold_in(key, 1), S_ENC, S_ENC, HD)[0].astype(jnp.bfloat16)


def draw_enc_key(key, part):
    return paired(jax.random.fold_in(key, 1), S_ENC, S_ENC, HD)[1].astype(jnp.bfloat16)


def draw_dec_query(key, part):
    return paired(jax.random.fold_in(key, 2), T_DEC, S_ENC, HD)[0].astype(jnp.bfloat16)


def draw_cross_key(key, part):
    return paired(jax.random.fold_in(key, 2), T_DEC, S_ENC, HD)[1].astype(jnp.bfloat16)


def shard_levels(own_key, dims, cuts, least, top_value):
    level, own = 1.0, jax.random.fold_in(own_key, 6)
    for axis_at, shards_of in cuts:
        draws = jnp.exp(jax.random.uniform(jax.random.fold_in(own, axis_at), (shards_of,), jnp.float32, least / len(cuts), top_value / len(cuts)))
        level = level * jnp.repeat(draws, dims[axis_at] // shards_of).reshape([-1 if axis == axis_at else 1 for axis in range(len(dims))])
    return level


def gaussian(own_key, shape, deviation, reach, shards=(), dtype=jnp.bfloat16):
    array = jax.random.normal(own_key, shape, jnp.float32) * deviation
    if len(shards) > 0:
        array = shard_levels(own_key, shape, shards, -0.22, 0.18) * array
    return jnp.clip(array, min=-reach, max=reach).astype(dtype)


def setup_inputs(seed: int = 0) -> dict:
    keys = jax.random.split(jax.random.key(seed), 7)
    enc_query = draw_enc_query(jax.random.fold_in(keys[6], 71), 0)
    enc_key = draw_enc_key(jax.random.fold_in(keys[6], 71), 0)
    enc_value = gaussian(keys[2], (S_ENC, HD), 1.0, 6.0, ((0, 512),))
    dec_query = draw_dec_query(jax.random.fold_in(keys[6], 71), 0)
    cross_key = draw_cross_key(jax.random.fold_in(keys[6], 71), 0)
    cross_value = gaussian(keys[5], (S_ENC, HD), 1.0, 6.0, ((0, 512),))
    return {"enc_query": enc_query, "enc_key": enc_key, "enc_value": enc_value, "dec_query": dec_query, "cross_key": cross_key, "cross_value": cross_value}


def attend(queries, key_rows, values):
    score_scale = HEAD_DIM ** -0.5
    query_heads = jnp.moveaxis(queries.reshape(queries.shape[0], HEADS, HEAD_DIM), 1, 0)
    key_heads = jnp.moveaxis(key_rows.reshape(key_rows.shape[0], HEADS, HEAD_DIM), 1, 0)
    value_heads = jnp.moveaxis(values.reshape(values.shape[0], HEADS, HEAD_DIM), 1, 0)

    def single_head(operands):
        query_block, key_block, value_block = operands
        scores = jnp.dot(query_block, key_block.T, preferred_element_type=jnp.float32) * score_scale
        row_top = jnp.max(scores, axis=1, keepdims=True)
        weights = jnp.exp(scores - row_top)
        row_total = jnp.sum(weights, axis=1, keepdims=True)
        mixed_values = jnp.dot(weights.astype(jnp.bfloat16), value_block, preferred_element_type=jnp.float32)
        return (mixed_values / row_total).astype(jnp.bfloat16)

    results = lax.map(single_head, (query_heads, key_heads, value_heads))
    return jnp.moveaxis(results, 0, 1).reshape(queries.shape[0], HEADS * HEAD_DIM)


def reference(enc_query, enc_key, enc_value, dec_query, cross_key, cross_value):
    enc_context = attend(enc_query, enc_key, enc_value)
    dec_context = attend(dec_query, cross_key, cross_value)
    return (enc_context, dec_context)
```

```python
import jax
import jax.numpy as jnp
from jax import lax
from jax.sharding import PartitionSpec as P

HEAD_DIM = 128


def absorb(partial_state, query_block, key_block, value_block):
    row_top, row_total, weighted = partial_state
    head_count = query_block.shape[1] // HEAD_DIM
    query_heads = query_block.reshape(query_block.shape[0], head_count, HEAD_DIM)
    key_heads = key_block.reshape(key_block.shape[0], head_count, HEAD_DIM)
    value_heads = value_block.reshape(value_block.shape[0], head_count, HEAD_DIM)
    scores = jnp.einsum(
        "qhd,khd->hqk", query_heads, key_heads, preferred_element_type=jnp.float32
    ) * HEAD_DIM ** (-0.5)
    new_top = jnp.maximum(row_top, jnp.max(scores, axis=2))
    shrink = jnp.exp(row_top - new_top)
    weights = jnp.exp(scores - new_top[:, :, None])
    row_total = row_total * shrink + jnp.sum(weights, axis=2)
    mixed_values = jnp.einsum(
        "hqk,khd->qhd",
        weights.astype(jnp.bfloat16),
        value_heads,
        preferred_element_type=jnp.float32,
    )
    weighted = weighted * jnp.transpose(shrink)[:, :, None] + mixed_values
    return (new_top, row_total, weighted)


def empty_state(row_count, columns):
    head_count = columns // HEAD_DIM
    return (
        jnp.full((head_count, row_count), -1e30, jnp.float32),
        jnp.zeros((head_count, row_count), jnp.float32),
        jnp.zeros((row_count, head_count, HEAD_DIM), jnp.float32),
    )


def finish(partial_state):
    row_top, row_total, weighted = partial_state
    normed = weighted / jnp.transpose(row_total)[:, :, None]
    return normed.reshape(weighted.shape[0], -1).astype(jnp.bfloat16)


def shards(enc_query, enc_key, enc_value, dec_query, cross_key, cross_value):
    local_query, local_key, local_value, visitor, resident_key, resident_value = (
        lax.all_to_all(enc_query, "tp", split_axis=1, concat_axis=0, tiled=True),
        lax.all_to_all(enc_key, "tp", split_axis=1, concat_axis=0, tiled=True),
        lax.all_to_all(enc_value, "tp", split_axis=1, concat_axis=0, tiled=True),
        lax.all_to_all(dec_query, "tp", split_axis=1, concat_axis=0, tiled=True),
        lax.all_to_all(cross_key, "tp", split_axis=1, concat_axis=0, tiled=True),
        lax.all_to_all(cross_value, "tp", split_axis=1, concat_axis=0, tiled=True),
    )
    enc_state = absorb(
        empty_state(local_query.shape[0], local_query.shape[1]),
        local_query,
        lax.all_gather(local_key, "ctx", axis=0, tiled=True),
        lax.all_gather(local_value, "ctx", axis=0, tiled=True),
    )
    enc_context = finish(enc_state)

    ring = lax.axis_size("ctx")
    rows, columns = visitor.shape
    heads = columns // HEAD_DIM
    every_query = lax.all_gather(visitor, "ctx", axis=0, tiled=True)
    row_top, row_total, weighted = absorb(
        empty_state(rows * ring, columns), every_query, resident_key, resident_value
    )
    stats = jnp.stack([row_top.T, row_total.T], axis=1).reshape(ring, rows, 2 * heads)
    sums = weighted.reshape(ring, rows, columns).astype(jnp.bfloat16)
    stats = lax.all_to_all(stats, "ctx", split_axis=0, concat_axis=0, tiled=True)
    sums = lax.all_to_all(sums, "ctx", split_axis=0, concat_axis=0, tiled=True)
    stats = stats.reshape(ring, rows, 2, heads)
    tops, totals = stats[:, :, 0], stats[:, :, 1]
    scale = jnp.exp(tops - jnp.max(tops, axis=0, keepdims=True))
    total = jnp.sum(scale * totals, axis=0)
    mixed = jnp.sum(scale[..., None] * sums.reshape(ring, rows, heads, HEAD_DIM).astype(jnp.float32), axis=0)
    dec_context = (mixed / total[..., None]).reshape(rows, columns).astype(jnp.bfloat16)
    return (enc_context, dec_context)


def solution(mesh):
    in_specs = (
        P(("ctx", "tp"), None),
        P(("ctx", "tp"), None),
        P(("ctx", "tp"), None),
        P(("ctx", "tp"), None),
        P(("ctx", "tp"), None),
        P(("ctx", "tp"), None),
    )
    out_specs = (P("ctx", "tp"), P("ctx", "tp"))
    return jax.shard_map(shards, mesh=mesh, in_specs=in_specs, out_specs=out_specs, check_vma=False)
```

```python
import functools

import jax
import jax.numpy as jnp
from jax import lax
from jax.experimental import pallas as pl
from jax.experimental.pallas import tpu as pltpu
from jax.sharding import PartitionSpec as P

HEAD_DIM = 128
RING = 8
LOG2E = 1.4426950408889634
STEEP = HEAD_DIM ** (-0.5) * LOG2E
MESH = pl.DeviceIdType.MESH
KEY_RIGHT = (1, 2, 3, 4)
VALUE_RIGHT = (1, 2, 3)


def scores_of(query, key):
    return lax.dot_general(query, key, (((1,), (1,)), ((), ())), preferred_element_type=jnp.float32)


def kernel(
    q_ref, k_ref, v_ref, dq_ref, ck_ref, cv_ref, enc_ref, dec_ref,
    qb, kb, vb, db, ckb, cvb, top, total, acc, estat, dstat,
    esend, esend_stat, eback, eback_stat, psend, psend_stat, pback, pback_stat,
    wide, zsend, zsend_stat, zback, zback_stat, dmix,
    ks, kr, vs, vr, ds, dr, kps, kpr, vps, vpr, rs, rr, rts, rtr, ms, mr, local,
):
    rows, columns = q_ref.shape
    drows = dq_ref.shape[0]
    heads = columns // HEAD_DIM
    me = lax.axis_index("ctx")
    plane, y, core = me // (2 * RING), (me // 2) % RING, me % 2

    def along(offset):
        return {"ctx": plane * (2 * RING) + lax.rem(y + offset + RING, RING) * 2 + core}

    twin = {"ctx": plane * (2 * RING) + y * 2 + (1 - core)}
    mirror = {"ctx": (1 - plane) * (2 * RING) + y * 2 + core}

    barrier = pltpu.get_barrier_semaphore()
    for peer in [along(offset) for offset in range(1, RING)] + [twin, mirror]:
        pl.semaphore_signal(barrier, inc=1, device_id=peer, device_id_type=MESH)
    pl.semaphore_wait(barrier, RING + 1)

    started = []

    def send(source, target, send_sem, recv_sem, device):
        copy = pltpu.make_async_remote_copy(
            src_ref=source, dst_ref=target, send_sem=send_sem, recv_sem=recv_sem,
            device_id=device, device_id_type=MESH,
        )
        copy.start()
        started.append(copy)

    def arrived(target, recv_sem):
        pltpu.make_async_remote_copy(
            src_ref=target, dst_ref=target, send_sem=recv_sem, recv_sem=recv_sem,
            device_id=twin, device_id_type=MESH,
        ).wait_recv()

    def onward(source, slot, buffer, send_sems, recv_sems, right):
        after, before = (slot + 1) % RING, (slot - 1) % RING
        if after in right:
            send(source, buffer(after), send_sems.at[after], recv_sems.at[after], along(1))
        if before not in right and before != 0:
            send(source, buffer(before), send_sems.at[before], recv_sems.at[before], along(-1))

    def pass_on(source, slot, buffer, send_sems, recv_sems, right):
        if slot == 0:
            onward(source, 0, buffer, send_sems, recv_sems, right)
        elif slot in right:
            if slot + 1 in right:
                send(source, buffer(slot + 1), send_sems.at[slot + 1], recv_sems.at[slot + 1], along(1))
        elif slot - 1 not in right and slot - 1 != 0:
            send(source, buffer(slot - 1), send_sems.at[slot - 1], recv_sems.at[slot - 1], along(-1))

    def key_slot(slot):
        return kb.at[slot, 0]

    def value_slot(slot):
        return vb.at[slot, 0]

    def query_slot(slot):
        return db.at[slot]

    send(dq_ref, db.at[0, 1], ms.at[0], mr.at[0], mirror)
    pass_on(k_ref, 0, key_slot, ks, kr, KEY_RIGHT)
    pass_on(v_ref, 0, value_slot, vs, vr, VALUE_RIGHT)
    send(k_ref, kb.at[0, 1], kps.at[0], kpr.at[0], twin)
    send(v_ref, vb.at[0, 1], vps.at[0], vpr.at[0], twin)
    send(q_ref, qb.at[1], ms.at[1], mr.at[1], mirror)
    send(ck_ref, ckb.at[1], ms.at[2], mr.at[2], twin)
    send(cv_ref, cvb.at[1], ms.at[3], mr.at[3], twin)
    own = pltpu.make_async_copy(dq_ref, db.at[0, 0], local)
    own.start()
    kb[0, 0] = k_ref[...]
    vb[0, 0] = v_ref[...]
    qb[0] = q_ref[...]
    ckb[0] = ck_ref[...]
    cvb[0] = cv_ref[...]
    own.wait()
    arrived(db.at[0, 1], mr.at[0])
    pass_on(db.at[0], 0, query_slot, ds, dr, KEY_RIGHT)
    estat[...] = jnp.zeros_like(estat)
    dstat[...] = jnp.zeros_like(dstat)
    wide[...] = jnp.zeros_like(wide)

    def attend(slots, first):
        def body(item, carry):
            half, head = item // heads, item % heads
            at = pl.ds(pl.multiple_of(head * HEAD_DIM, HEAD_DIM), HEAD_DIM)
            query = qb[half, :, at]
            parts = [scores_of(query, kb[slot, :, :, at].reshape(2 * rows, HEAD_DIM)) for slot in slots]
            new_top = functools.reduce(jnp.maximum, [jnp.max(part, axis=1, keepdims=True) for part in parts])
            if not first:
                new_top = jnp.maximum(new_top, top[item])
            mixed, summed = None, None
            for slot, part in zip(slots, parts):
                weights = jnp.exp2((part - new_top) * STEEP)
                one = jnp.sum(weights, axis=1, keepdims=True)
                two = jnp.dot(
                    weights.astype(jnp.bfloat16),
                    vb[slot, :, :, at].reshape(2 * rows, HEAD_DIM),
                    preferred_element_type=jnp.float32,
                )
                summed = one if summed is None else summed + one
                mixed = two if mixed is None else mixed + two
            if not first:
                shrink = jnp.exp2((top[item] - new_top) * STEEP)
                summed = summed + total[item] * shrink
                mixed = mixed + acc[item] * shrink
            top[item] = new_top
            total[item] = summed
            acc[item] = mixed
            return carry

        lax.fori_loop(0, 2 * heads, body, 0)

    def visit(slot):
        def body(head, carry):
            at = pl.ds(pl.multiple_of(head * HEAD_DIM, HEAD_DIM), HEAD_DIM)
            query = db[slot, :, :, at].reshape(2 * drows, HEAD_DIM)
            part = scores_of(query, ckb[:, :, at].reshape(2 * rows, HEAD_DIM))
            row_top = jnp.max(part, axis=1, keepdims=True)
            weights = jnp.exp2((part - row_top) * STEEP)
            summed = jnp.sum(weights, axis=1, keepdims=True)
            mixed = jnp.dot(
                weights.astype(jnp.bfloat16), cvb[:, :, at].reshape(2 * rows, HEAD_DIM),
                preferred_element_type=jnp.float32,
            )
            psend[slot, :, at] = mixed.astype(jnp.bfloat16)
            lane = lax.broadcasted_iota(jnp.int32, (2 * drows, HEAD_DIM), 1)
            held = dstat[0 : 2 * drows, :]
            held = jnp.where(lane == head, row_top, held)
            dstat[0 : 2 * drows, :] = jnp.where(lane == heads + head, summed, held)
            return carry

        lax.fori_loop(0, heads, body, 0)
        psend_stat[slot] = jnp.transpose(dstat[...])[0:8]
        if slot > 0:
            send(psend.at[slot], pback.at[slot], rs.at[slot], rr.at[slot], along(-slot))
            send(psend_stat.at[slot], pback_stat.at[slot], rts.at[slot], rtr.at[slot], along(-slot))
        else:
            pback[0] = psend[0]
            pback_stat[0] = psend_stat[0]

    arrived(kb.at[0, 1], kpr.at[0])
    arrived(vb.at[0, 1], vpr.at[0])
    arrived(qb.at[1], mr.at[1])
    attend((0,), True)
    arrived(ckb.at[1], mr.at[2])
    arrived(cvb.at[1], mr.at[3])
    visit(0)

    for step in range(1, RING // 2 + 1):
        pair = (step,) if step == RING - step else (step, RING - step)
        for slot in pair:
            arrived(kb.at[slot, 0], kr.at[slot])
            pass_on(kb.at[slot, 0], slot, key_slot, ks, kr, KEY_RIGHT)
            send(kb.at[slot, 0], kb.at[slot, 1], kps.at[slot], kpr.at[slot], twin)
        for slot in pair:
            arrived(vb.at[slot, 0], vr.at[slot])
            pass_on(vb.at[slot, 0], slot, value_slot, vs, vr, VALUE_RIGHT)
            send(vb.at[slot, 0], vb.at[slot, 1], vps.at[slot], vpr.at[slot], twin)
        for slot in pair:
            arrived(db.at[slot], dr.at[slot])
            pass_on(db.at[slot], slot, query_slot, ds, dr, KEY_RIGHT)
        for slot in pair:
            visit(slot)
        for slot in pair:
            arrived(kb.at[slot, 1], kpr.at[slot])
            arrived(vb.at[slot, 1], vpr.at[slot])
        attend(pair, False)

    lane = lax.broadcasted_iota(jnp.int32, (rows, HEAD_DIM), 1)
    held = jnp.zeros((rows, HEAD_DIM), jnp.float32)
    for head in range(heads):
        item = heads + head
        esend[:, head * HEAD_DIM : (head + 1) * HEAD_DIM] = acc[item].astype(jnp.bfloat16)
        held = jnp.where(lane == head, top[item], held)
        held = jnp.where(lane == heads + head, total[item], held)
    estat[0:rows, :] = held
    for chunk in range(2):
        esend_stat[chunk] = jnp.transpose(estat[chunk * 128 : (chunk + 1) * 128, :])[0:8]
    send(esend, eback, ms.at[4], mr.at[4], mirror)
    send(esend_stat, eback_stat, ms.at[5], mr.at[5], mirror)

    for slot in range(1, RING):
        arrived(pback.at[slot], rr.at[slot])
        arrived(pback_stat.at[slot], rtr.at[slot])
    stats = [pback_stat[slot] for slot in range(RING)]
    best = functools.reduce(jnp.maximum, [stat[0:heads] for stat in stats])
    joined = None
    for slot in range(RING):
        weight = jnp.exp2((stats[slot][0:heads] - best) * STEEP)
        wide[slot * 8 : slot * 8 + heads, :] = weight
        term = weight * stats[slot][heads : 2 * heads]
        joined = term if joined is None else joined + term
    zsend_stat[...] = jnp.zeros_like(zsend_stat)
    zsend_stat[0:heads, :] = best
    zsend_stat[heads : 2 * heads, :] = joined
    turned = jnp.transpose(wide[...])
    for head in range(heads):
        span = slice(head * HEAD_DIM, (head + 1) * HEAD_DIM)
        mixed = None
        for slot in range(RING):
            term = pback[slot, :, span].astype(jnp.float32) * turned[0 : 2 * drows, slot * 8 + head : slot * 8 + head + 1]
            mixed = term if mixed is None else mixed + term
        dmix[:, span] = mixed
        zsend[:, span] = mixed[drows:].astype(jnp.bfloat16)
    send(zsend, zback, ms.at[6], mr.at[6], mirror)
    send(zsend_stat, zback_stat, ms.at[7], mr.at[7], mirror)

    arrived(eback, mr.at[4])
    arrived(eback_stat, mr.at[5])
    wide[8:, :] = jnp.zeros((120, 128), jnp.float32)
    for chunk in range(2):
        wide[0:8, :] = eback_stat[chunk]
        estat[chunk * 128 : (chunk + 1) * 128, :] = jnp.transpose(wide[...])
    for head in range(heads):
        span = slice(head * HEAD_DIM, (head + 1) * HEAD_DIM)
        other_top = estat[0:rows, head : head + 1]
        other_total = estat[0:rows, heads + head : heads + head + 1]
        peak = jnp.maximum(top[head], other_top)
        mine = jnp.exp2((top[head] - peak) * STEEP)
        theirs = jnp.exp2((other_top - peak) * STEEP)
        whole = mine * acc[head] + theirs * eback[:, span].astype(jnp.float32)
        enc_ref[:, span] = (whole / (mine * total[head] + theirs * other_total)).astype(jnp.bfloat16)

    arrived(zback, mr.at[6])
    arrived(zback_stat, mr.at[7])
    wide[0:8, :] = zsend_stat[...]
    wide[8:16, :] = zback_stat[...]
    turned = jnp.transpose(wide[...])
    for head in range(heads):
        span = slice(head * HEAD_DIM, (head + 1) * HEAD_DIM)
        own_top = turned[0:drows, head : head + 1]
        own_total = turned[0:drows, heads + head : heads + head + 1]
        other_top = turned[drows : 2 * drows, 8 + head : 8 + head + 1]
        other_total = turned[drows : 2 * drows, 8 + heads + head : 8 + heads + head + 1]
        peak = jnp.maximum(own_top, other_top)
        mine = jnp.exp2((own_top - peak) * STEEP)
        theirs = jnp.exp2((other_top - peak) * STEEP)
        whole = mine * dmix[0:drows, span] + theirs * zback[:, span].astype(jnp.float32)
        dec_ref[:, span] = (whole / (mine * own_total + theirs * other_total)).astype(jnp.bfloat16)

    for copy in started:
        copy.wait_send()


def attention(query, key, value, dec_query, cross_key, cross_value):
    rows, columns = query.shape
    drows = dec_query.shape[0]
    heads = columns // HEAD_DIM
    bf16, f32 = jnp.bfloat16, jnp.float32
    vmem = pl.BlockSpec(memory_space=pltpu.VMEM)
    eight = pltpu.SemaphoreType.DMA((RING,))
    return pl.pallas_call(
        kernel,
        out_shape=(
            jax.ShapeDtypeStruct((rows, columns), bf16),
            jax.ShapeDtypeStruct((drows, columns), bf16),
        ),
        in_specs=[vmem] * 6,
        out_specs=(vmem, vmem),
        scratch_shapes=[
            pltpu.VMEM((2, rows, columns), bf16),
            pltpu.VMEM((RING, 2, rows, columns), bf16),
            pltpu.VMEM((RING, 2, rows, columns), bf16),
            pltpu.VMEM((RING, 2, drows, columns), bf16),
            pltpu.VMEM((2, rows, columns), bf16),
            pltpu.VMEM((2, rows, columns), bf16),
            pltpu.VMEM((2 * heads, rows, 1), f32),
            pltpu.VMEM((2 * heads, rows, 1), f32),
            pltpu.VMEM((2 * heads, rows, HEAD_DIM), f32),
            pltpu.VMEM((256, 128), f32),
            pltpu.VMEM((128, 128), f32),
            pltpu.VMEM((rows, columns), bf16),
            pltpu.VMEM((2, 8, 128), f32),
            pltpu.VMEM((rows, columns), bf16),
            pltpu.VMEM((2, 8, 128), f32),
            pltpu.VMEM((RING, 2 * drows, columns), bf16),
            pltpu.VMEM((RING, 8, 128), f32),
            pltpu.VMEM((RING, 2 * drows, columns), bf16),
            pltpu.VMEM((RING, 8, 128), f32),
            pltpu.VMEM((128, 128), f32),
            pltpu.VMEM((drows, columns), bf16),
            pltpu.VMEM((8, 128), f32),
            pltpu.VMEM((drows, columns), bf16),
            pltpu.VMEM((8, 128), f32),
            pltpu.VMEM((2 * drows, columns), f32),
        ]
        + [eight] * 16
        + [pltpu.SemaphoreType.DMA],
        compiler_params=pltpu.CompilerParams(
            collective_id=0, has_side_effects=True, vmem_limit_bytes=40 << 20
        ),
    )(query, key, value, dec_query, cross_key, cross_value)


def shards(enc_query, enc_key, enc_value, dec_query, cross_key, cross_value):
    arrays = (enc_key, enc_value, enc_query, cross_key, cross_value, dec_query)
    packed = jnp.concatenate(arrays, axis=0)
    count, columns = packed.shape
    tp = lax.axis_size("tp")
    packed = packed.reshape(count, tp, columns // tp).transpose(1, 0, 2)
    packed = lax.all_to_all(packed, "tp", split_axis=0, concat_axis=0, tiled=True)
    pieces, start = [], 0
    for array in arrays:
        piece = packed[:, start : start + array.shape[0]]
        pieces.append(piece.reshape(tp * array.shape[0], columns // tp))
        start += array.shape[0]
    key, value, query, ckey, cvalue, dquery = pieces
    return attention(query, key, value, dquery, ckey, cvalue)


def solution(mesh):
    in_specs = (P(("ctx", "tp"), None),) * 6
    out_specs = (P("ctx", "tp"), P("ctx", "tp"))
    return jax.shard_map(shards, mesh=mesh, in_specs=in_specs, out_specs=out_specs, check_vma=False)
```

```python
import functools

import jax
import jax.numpy as jnp
from jax import lax
from jax.experimental import pallas as pl
from jax.experimental.pallas import tpu as pltpu
from jax.sharding import PartitionSpec as P

HEAD_DIM = 128
RING = 8
LOG2E = 1.4426950408889634
STEEP = HEAD_DIM ** (-0.5) * LOG2E
MESH = pl.DeviceIdType.MESH
KEY_RIGHT = (1, 2, 3, 4)
VALUE_RIGHT = (1, 2, 3)


def scores_of(query, key):
    return lax.dot_general(query, key, (((1,), (1,)), ((), ())), preferred_element_type=jnp.float32)


def kernel(
    q_arg, k_arg, v_arg, dq_arg, ck_arg, cv_arg, enc_ref, dec_ref,
    q_parts, k_parts, v_parts, dq_parts, ck_parts, cv_parts,
    dq_ref, qb, kb, vb, db, ckb, cvb, top, total, acc, estat, dstat,
    esend, esend_stat, eback, eback_stat, psend, psend_stat, pback, pback_stat,
    wide, zsend, zsend_stat, zback, zback_stat, dmix,
    ks, kr, vs, vr, ds, dr, kps, kpr, vps, vpr, rs, rr, rts, rtr, ms, mr, ts, tr, self_sems,
):
    rows, columns = enc_ref.shape
    drows = dq_ref.shape[0]
    tokens = q_arg.shape[0]
    dtokens = dq_arg.shape[0]
    group = q_parts.shape[0]
    here = lax.axis_index("tp")
    heads = columns // HEAD_DIM
    me = lax.axis_index("ctx")
    plane, y, core = me // (2 * RING), (me // 2) % RING, me % 2

    def along(offset):
        return {"ctx": plane * (2 * RING) + lax.rem(y + offset + RING, RING) * 2 + core}

    twin = {"ctx": plane * (2 * RING) + y * 2 + (1 - core)}
    mirror = {"ctx": (1 - plane) * (2 * RING) + y * 2 + core}

    barrier = pltpu.get_barrier_semaphore()
    for peer in [along(offset) for offset in range(1, RING)] + [twin, mirror]:
        pl.semaphore_signal(barrier, inc=1, device_id=peer, device_id_type=MESH)
    for offset in range(1, group):
        pl.semaphore_signal(
            barrier, inc=1, device_id={"tp": lax.rem(here + offset, group)}, device_id_type=MESH
        )
    pl.semaphore_wait(barrier, RING + group)

    started = []

    def send(source, target, send_sem, recv_sem, device):
        copy = pltpu.make_async_remote_copy(
            src_ref=source, dst_ref=target, send_sem=send_sem, recv_sem=recv_sem,
            device_id=device, device_id_type=MESH,
        )
        copy.start()
        started.append(copy)

    def arrived(target, recv_sem):
        pltpu.make_async_remote_copy(
            src_ref=target, dst_ref=target, send_sem=recv_sem, recv_sem=recv_sem,
            device_id=twin, device_id_type=MESH,
        ).wait_recv()

    def onward(source, slot, buffer, send_sems, recv_sems, right):
        after, before = (slot + 1) % RING, (slot - 1) % RING
        if after in right:
            send(source, buffer(after), send_sems.at[after], recv_sems.at[after], along(1))
        if before not in right and before != 0:
            send(source, buffer(before), send_sems.at[before], recv_sems.at[before], along(-1))

    def pass_on(source, slot, buffer, send_sems, recv_sems, right):
        if slot == 0:
            onward(source, 0, buffer, send_sems, recv_sems, right)
        elif slot in right:
            if slot + 1 in right:
                send(source, buffer(slot + 1), send_sems.at[slot + 1], recv_sems.at[slot + 1], along(1))
        elif slot - 1 not in right and slot - 1 != 0:
            send(source, buffer(slot - 1), send_sems.at[slot - 1], recv_sems.at[slot - 1], along(-1))

    def key_slot(slot):
        return kb.at[slot, 0]

    def value_slot(slot):
        return vb.at[slot, 0]

    def query_slot(slot):
        return db.at[slot]

    exchanges = (
        (dq_arg, dq_parts), (k_arg, k_parts), (v_arg, v_parts),
        (q_arg, q_parts), (ck_arg, ck_parts), (cv_arg, cv_parts),
    )

    def slab(which, peer):
        argument, parts = exchanges[which]
        return argument.at[:, pl.ds(pl.multiple_of(peer * columns, 128), columns)]

    def slab_copy(which, offset):
        peer = lax.rem(here + offset, group)
        return pltpu.make_async_remote_copy(
            src_ref=slab(which, peer), dst_ref=exchanges[which][1].at[here],
            send_sem=ts.at[which, offset], recv_sem=tr.at[which, here],
            device_id={"tp": peer}, device_id_type=MESH,
        )

    def self_copy(which):
        return pltpu.make_async_copy(slab(which, here), exchanges[which][1].at[here], self_sems.at[which])

    for which in range(6):
        self_copy(which).start()

        def start_one(offset, carry):
            slab_copy(which, offset).start()
            return carry

        lax.fori_loop(1, group, start_one, 0)

    def gather(which):
        parts = exchanges[which][1]

        def wait_one(offset, carry):
            origin = lax.rem(here + offset, group)
            pltpu.make_async_remote_copy(
                src_ref=parts.at[origin], dst_ref=parts.at[origin],
                send_sem=ts.at[which, offset], recv_sem=tr.at[which, origin],
                device_id=twin, device_id_type=MESH,
            ).wait_recv()
            return carry

        lax.fori_loop(1, group, wait_one, 0)
        self_copy(which).wait()
        return parts

    parts = gather(0)
    for source in range(group):
        piece = parts[source]
        dq_ref[source * dtokens : (source + 1) * dtokens, :] = piece
        db[0, 0, source * dtokens : (source + 1) * dtokens, :] = piece
    send(dq_ref, db.at[0, 1], ms.at[0], mr.at[0], mirror)
    parts = gather(1)
    for source in range(group):
        kb[0, 0, source * tokens : (source + 1) * tokens, :] = parts[source]
    pass_on(kb.at[0, 0], 0, key_slot, ks, kr, KEY_RIGHT)
    send(kb.at[0, 0], kb.at[0, 1], kps.at[0], kpr.at[0], twin)
    parts = gather(2)
    for source in range(group):
        vb[0, 0, source * tokens : (source + 1) * tokens, :] = parts[source]
    pass_on(vb.at[0, 0], 0, value_slot, vs, vr, VALUE_RIGHT)
    send(vb.at[0, 0], vb.at[0, 1], vps.at[0], vpr.at[0], twin)
    arrived(db.at[0, 1], mr.at[0])
    pass_on(db.at[0], 0, query_slot, ds, dr, KEY_RIGHT)
    parts = gather(3)
    for source in range(group):
        qb[0, source * tokens : (source + 1) * tokens, :] = parts[source]
    send(qb.at[0], qb.at[1], ms.at[1], mr.at[1], mirror)
    parts = gather(4)
    for source in range(group):
        ckb[0, source * tokens : (source + 1) * tokens, :] = parts[source]
    send(ckb.at[0], ckb.at[1], ms.at[2], mr.at[2], twin)
    parts = gather(5)
    for source in range(group):
        cvb[0, source * tokens : (source + 1) * tokens, :] = parts[source]
    send(cvb.at[0], cvb.at[1], ms.at[3], mr.at[3], twin)
    estat[...] = jnp.zeros_like(estat)
    dstat[...] = jnp.zeros_like(dstat)
    wide[...] = jnp.zeros_like(wide)

    def attend(slots, first):
        def body(item, carry):
            half, head = item // heads, item % heads
            at = pl.ds(pl.multiple_of(head * HEAD_DIM, HEAD_DIM), HEAD_DIM)
            query = qb[half, :, at]
            parts = [scores_of(query, kb[slot, :, :, at].reshape(2 * rows, HEAD_DIM)) for slot in slots]
            new_top = functools.reduce(jnp.maximum, [jnp.max(part, axis=1, keepdims=True) for part in parts])
            if not first:
                new_top = jnp.maximum(new_top, top[item])
            mixed, summed = None, None
            for slot, part in zip(slots, parts):
                weights = jnp.exp2((part - new_top) * STEEP)
                one = jnp.sum(weights, axis=1, keepdims=True)
                two = jnp.dot(
                    weights.astype(jnp.bfloat16),
                    vb[slot, :, :, at].reshape(2 * rows, HEAD_DIM),
                    preferred_element_type=jnp.float32,
                )
                summed = one if summed is None else summed + one
                mixed = two if mixed is None else mixed + two
            if not first:
                shrink = jnp.exp2((top[item] - new_top) * STEEP)
                summed = summed + total[item] * shrink
                mixed = mixed + acc[item] * shrink
            top[item] = new_top
            total[item] = summed
            acc[item] = mixed
            return carry

        lax.fori_loop(0, 2 * heads, body, 0)

    def visit(slot):
        def body(head, carry):
            at = pl.ds(pl.multiple_of(head * HEAD_DIM, HEAD_DIM), HEAD_DIM)
            query = db[slot, :, :, at].reshape(2 * drows, HEAD_DIM)
            part = scores_of(query, ckb[:, :, at].reshape(2 * rows, HEAD_DIM))
            row_top = jnp.max(part, axis=1, keepdims=True)
            weights = jnp.exp2((part - row_top) * STEEP)
            summed = jnp.sum(weights, axis=1, keepdims=True)
            mixed = jnp.dot(
                weights.astype(jnp.bfloat16), cvb[:, :, at].reshape(2 * rows, HEAD_DIM),
                preferred_element_type=jnp.float32,
            )
            psend[slot, :, at] = mixed.astype(jnp.bfloat16)
            lane = lax.broadcasted_iota(jnp.int32, (2 * drows, HEAD_DIM), 1)
            held = dstat[0 : 2 * drows, :]
            held = jnp.where(lane == head, row_top, held)
            dstat[0 : 2 * drows, :] = jnp.where(lane == heads + head, summed, held)
            return carry

        lax.fori_loop(0, heads, body, 0)
        psend_stat[slot] = jnp.transpose(dstat[...])[0:8]
        if slot > 0:
            send(psend.at[slot], pback.at[slot], rs.at[slot], rr.at[slot], along(-slot))
            send(psend_stat.at[slot], pback_stat.at[slot], rts.at[slot], rtr.at[slot], along(-slot))
        else:
            pback[0] = psend[0]
            pback_stat[0] = psend_stat[0]

    arrived(kb.at[0, 1], kpr.at[0])
    arrived(vb.at[0, 1], vpr.at[0])
    arrived(qb.at[1], mr.at[1])
    attend((0,), True)
    arrived(ckb.at[1], mr.at[2])
    arrived(cvb.at[1], mr.at[3])
    visit(0)

    for step in range(1, RING // 2 + 1):
        pair = (step,) if step == RING - step else (step, RING - step)
        for slot in pair:
            arrived(kb.at[slot, 0], kr.at[slot])
            pass_on(kb.at[slot, 0], slot, key_slot, ks, kr, KEY_RIGHT)
            send(kb.at[slot, 0], kb.at[slot, 1], kps.at[slot], kpr.at[slot], twin)
        for slot in pair:
            arrived(vb.at[slot, 0], vr.at[slot])
            pass_on(vb.at[slot, 0], slot, value_slot, vs, vr, VALUE_RIGHT)
            send(vb.at[slot, 0], vb.at[slot, 1], vps.at[slot], vpr.at[slot], twin)
        for slot in pair:
            arrived(db.at[slot], dr.at[slot])
            pass_on(db.at[slot], slot, query_slot, ds, dr, KEY_RIGHT)
        for slot in pair:
            visit(slot)
        for slot in pair:
            arrived(kb.at[slot, 1], kpr.at[slot])
            arrived(vb.at[slot, 1], vpr.at[slot])
        attend(pair, False)

    lane = lax.broadcasted_iota(jnp.int32, (rows, HEAD_DIM), 1)
    held = jnp.zeros((rows, HEAD_DIM), jnp.float32)
    for head in range(heads):
        item = heads + head
        esend[:, head * HEAD_DIM : (head + 1) * HEAD_DIM] = acc[item].astype(jnp.bfloat16)
        held = jnp.where(lane == head, top[item], held)
        held = jnp.where(lane == heads + head, total[item], held)
    estat[0:rows, :] = held
    for chunk in range(2):
        esend_stat[chunk] = jnp.transpose(estat[chunk * 128 : (chunk + 1) * 128, :])[0:8]
    send(esend, eback, ms.at[4], mr.at[4], mirror)
    send(esend_stat, eback_stat, ms.at[5], mr.at[5], mirror)

    for slot in range(1, RING):
        arrived(pback.at[slot], rr.at[slot])
        arrived(pback_stat.at[slot], rtr.at[slot])
    stats = [pback_stat[slot] for slot in range(RING)]
    best = functools.reduce(jnp.maximum, [stat[0:heads] for stat in stats])
    joined = None
    for slot in range(RING):
        weight = jnp.exp2((stats[slot][0:heads] - best) * STEEP)
        wide[slot * 8 : slot * 8 + heads, :] = weight
        term = weight * stats[slot][heads : 2 * heads]
        joined = term if joined is None else joined + term
    zsend_stat[...] = jnp.zeros_like(zsend_stat)
    zsend_stat[0:heads, :] = best
    zsend_stat[heads : 2 * heads, :] = joined
    turned = jnp.transpose(wide[...])
    for head in range(heads):
        span = slice(head * HEAD_DIM, (head + 1) * HEAD_DIM)
        mixed = None
        for slot in range(RING):
            term = pback[slot, :, span].astype(jnp.float32) * turned[0 : 2 * drows, slot * 8 + head : slot * 8 + head + 1]
            mixed = term if mixed is None else mixed + term
        dmix[:, span] = mixed
        zsend[:, span] = mixed[drows:].astype(jnp.bfloat16)
    send(zsend, zback, ms.at[6], mr.at[6], mirror)
    send(zsend_stat, zback_stat, ms.at[7], mr.at[7], mirror)

    arrived(eback, mr.at[4])
    arrived(eback_stat, mr.at[5])
    wide[8:, :] = jnp.zeros((120, 128), jnp.float32)
    for chunk in range(2):
        wide[0:8, :] = eback_stat[chunk]
        estat[chunk * 128 : (chunk + 1) * 128, :] = jnp.transpose(wide[...])
    for head in range(heads):
        span = slice(head * HEAD_DIM, (head + 1) * HEAD_DIM)
        other_top = estat[0:rows, head : head + 1]
        other_total = estat[0:rows, heads + head : heads + head + 1]
        peak = jnp.maximum(top[head], other_top)
        mine = jnp.exp2((top[head] - peak) * STEEP)
        theirs = jnp.exp2((other_top - peak) * STEEP)
        whole = mine * acc[head] + theirs * eback[:, span].astype(jnp.float32)
        enc_ref[:, span] = (whole / (mine * total[head] + theirs * other_total)).astype(jnp.bfloat16)

    arrived(zback, mr.at[6])
    arrived(zback_stat, mr.at[7])
    wide[0:8, :] = zsend_stat[...]
    wide[8:16, :] = zback_stat[...]
    turned = jnp.transpose(wide[...])
    for head in range(heads):
        span = slice(head * HEAD_DIM, (head + 1) * HEAD_DIM)
        own_top = turned[0:drows, head : head + 1]
        own_total = turned[0:drows, heads + head : heads + head + 1]
        other_top = turned[drows : 2 * drows, 8 + head : 8 + head + 1]
        other_total = turned[drows : 2 * drows, 8 + heads + head : 8 + heads + head + 1]
        peak = jnp.maximum(own_top, other_top)
        mine = jnp.exp2((own_top - peak) * STEEP)
        theirs = jnp.exp2((other_top - peak) * STEEP)
        whole = mine * dmix[0:drows, span] + theirs * zback[:, span].astype(jnp.float32)
        dec_ref[:, span] = (whole / (mine * own_total + theirs * other_total)).astype(jnp.bfloat16)

    for copy in started:
        copy.wait_send()
    for which in range(6):

        def drain_one(offset, carry):
            slab_copy(which, offset).wait_send()
            return carry

        lax.fori_loop(1, group, drain_one, 0)


def attention(query, key, value, dec_query, cross_key, cross_value):
    group = lax.axis_size("tp")
    tokens, dtokens = query.shape[0], dec_query.shape[0]
    rows, drows, columns = group * tokens, group * dtokens, query.shape[1] // group
    heads = columns // HEAD_DIM
    bf16, f32 = jnp.bfloat16, jnp.float32
    vmem = pl.BlockSpec(memory_space=pltpu.VMEM)
    eight = pltpu.SemaphoreType.DMA((RING,))
    return pl.pallas_call(
        kernel,
        out_shape=(
            jax.ShapeDtypeStruct((rows, columns), bf16),
            jax.ShapeDtypeStruct((drows, columns), bf16),
        ),
        in_specs=[pl.BlockSpec(memory_space=pl.ANY)] * 6,
        out_specs=(vmem, vmem),
        scratch_shapes=[
            pltpu.VMEM((group, tokens, columns), bf16),
            pltpu.VMEM((group, tokens, columns), bf16),
            pltpu.VMEM((group, tokens, columns), bf16),
            pltpu.VMEM((group, dtokens, columns), bf16),
            pltpu.VMEM((group, tokens, columns), bf16),
            pltpu.VMEM((group, tokens, columns), bf16),
            pltpu.VMEM((drows, columns), bf16),
            pltpu.VMEM((2, rows, columns), bf16),
            pltpu.VMEM((RING, 2, rows, columns), bf16),
            pltpu.VMEM((RING, 2, rows, columns), bf16),
            pltpu.VMEM((RING, 2, drows, columns), bf16),
            pltpu.VMEM((2, rows, columns), bf16),
            pltpu.VMEM((2, rows, columns), bf16),
            pltpu.VMEM((2 * heads, rows, 1), f32),
            pltpu.VMEM((2 * heads, rows, 1), f32),
            pltpu.VMEM((2 * heads, rows, HEAD_DIM), f32),
            pltpu.VMEM((256, 128), f32),
            pltpu.VMEM((128, 128), f32),
            pltpu.VMEM((rows, columns), bf16),
            pltpu.VMEM((2, 8, 128), f32),
            pltpu.VMEM((rows, columns), bf16),
            pltpu.VMEM((2, 8, 128), f32),
            pltpu.VMEM((RING, 2 * drows, columns), bf16),
            pltpu.VMEM((RING, 8, 128), f32),
            pltpu.VMEM((RING, 2 * drows, columns), bf16),
            pltpu.VMEM((RING, 8, 128), f32),
            pltpu.VMEM((128, 128), f32),
            pltpu.VMEM((drows, columns), bf16),
            pltpu.VMEM((8, 128), f32),
            pltpu.VMEM((drows, columns), bf16),
            pltpu.VMEM((8, 128), f32),
            pltpu.VMEM((2 * drows, columns), f32),
        ]
        + [eight] * 16
        + [pltpu.SemaphoreType.DMA((6, group))] * 2
        + [pltpu.SemaphoreType.DMA((6,))],
        compiler_params=pltpu.CompilerParams(
            collective_id=0, has_side_effects=True, vmem_limit_bytes=40 << 20
        ),
    )(query, key, value, dec_query, cross_key, cross_value)


def shards(enc_query, enc_key, enc_value, dec_query, cross_key, cross_value):
    return attention(enc_query, enc_key, enc_value, dec_query, cross_key, cross_value)


def solution(mesh):
    in_specs = (P(("ctx", "tp"), None),) * 6
    out_specs = (P("ctx", "tp"), P("ctx", "tp"))
    return jax.shard_map(shards, mesh=mesh, in_specs=in_specs, out_specs=out_specs, check_vma=False)
```

```python
import functools

import jax
import jax.numpy as jnp
from jax import lax
from jax.experimental import pallas as pl
from jax.experimental.pallas import tpu as pltpu
from jax.sharding import PartitionSpec as P

HEAD_DIM = 128
RING = 8
LOG2E = 1.4426950408889634
STEEP = HEAD_DIM ** (-0.5) * LOG2E
MESH = pl.DeviceIdType.MESH
KEY_RIGHT = (1, 2, 3, 4)
VALUE_RIGHT = (1, 2, 3)


def scores_of(query, key):
    return lax.dot_general(query, key, (((1,), (1,)), ((), ())), preferred_element_type=jnp.float32)


def kernel(
    q_arg, k_arg, v_arg, dq_arg, ck_arg, cv_arg, enc_ref, dec_ref,
    q_parts, k_parts, v_parts, dq_parts, ck_parts, cv_parts,
    dq_ref, qb, kb, vb, db, ckb, cvb, top, total, acc, estat, dstat,
    esend, esend_stat, eback, eback_stat, psend, psend_stat, pback, pback_stat,
    wide, zsend, zsend_stat, zback, zback_stat, dmix,
    ks, kr, vs, vr, ds, dr, kps, kpr, vps, vpr, rs, rr, rts, rtr, ms, mr, ts, tr, self_sems,
):
    rows, columns = enc_ref.shape
    drows = dq_ref.shape[0]
    tokens = q_arg.shape[0]
    dtokens = dq_arg.shape[0]
    group = q_parts.shape[0]
    here = lax.axis_index("tp")
    heads = columns // HEAD_DIM
    me = lax.axis_index("ctx")
    plane, y, core = me // (2 * RING), (me // 2) % RING, me % 2

    def along(offset):
        return {"ctx": plane * (2 * RING) + lax.rem(y + offset + RING, RING) * 2 + core}

    twin = {"ctx": plane * (2 * RING) + y * 2 + (1 - core)}
    mirror = {"ctx": (1 - plane) * (2 * RING) + y * 2 + core}

    barrier = pltpu.get_barrier_semaphore()
    for peer in [along(offset) for offset in range(1, RING)] + [twin, mirror]:
        pl.semaphore_signal(barrier, inc=1, device_id=peer, device_id_type=MESH)
    for offset in range(1, group):
        pl.semaphore_signal(
            barrier, inc=1, device_id={"tp": lax.rem(here + offset, group)}, device_id_type=MESH
        )
    pl.semaphore_wait(barrier, RING + group)

    started = []

    def send(source, target, send_sem, recv_sem, device):
        copy = pltpu.make_async_remote_copy(
            src_ref=source, dst_ref=target, send_sem=send_sem, recv_sem=recv_sem,
            device_id=device, device_id_type=MESH,
        )
        copy.start()
        started.append(copy)

    def arrived(target, recv_sem):
        pltpu.make_async_remote_copy(
            src_ref=target, dst_ref=target, send_sem=recv_sem, recv_sem=recv_sem,
            device_id=twin, device_id_type=MESH,
        ).wait_recv()

    def onward(source, slot, buffer, send_sems, recv_sems, right):
        after, before = (slot + 1) % RING, (slot - 1) % RING
        if after in right:
            send(source, buffer(after), send_sems.at[after], recv_sems.at[after], along(1))
        if before not in right and before != 0:
            send(source, buffer(before), send_sems.at[before], recv_sems.at[before], along(-1))

    def pass_on(source, slot, buffer, send_sems, recv_sems, right):
        if slot == 0:
            onward(source, 0, buffer, send_sems, recv_sems, right)
        elif slot in right:
            if slot + 1 in right:
                send(source, buffer(slot + 1), send_sems.at[slot + 1], recv_sems.at[slot + 1], along(1))
        elif slot - 1 not in right and slot - 1 != 0:
            send(source, buffer(slot - 1), send_sems.at[slot - 1], recv_sems.at[slot - 1], along(-1))

    def key_slot(slot):
        return kb.at[slot, 0]

    def value_slot(slot):
        return vb.at[slot, 0]

    def query_slot(slot):
        return db.at[slot]

    exchanges = (
        (dq_arg, dq_parts), (k_arg, k_parts), (v_arg, v_parts),
        (q_arg, q_parts), (ck_arg, ck_parts), (cv_arg, cv_parts),
    )

    def slab(which, peer):
        argument, parts = exchanges[which]
        return argument.at[:, pl.ds(pl.multiple_of(peer * columns, 128), columns)]

    def slab_copy(which, offset):
        peer = lax.rem(here + offset, group)
        return pltpu.make_async_remote_copy(
            src_ref=slab(which, peer), dst_ref=exchanges[which][1].at[here],
            send_sem=ts.at[which, offset], recv_sem=tr.at[which, here],
            device_id={"tp": peer}, device_id_type=MESH,
        )

    def self_copy(which):
        return pltpu.make_async_copy(slab(which, here), exchanges[which][1].at[here], self_sems.at[which])

    for which in range(6):
        self_copy(which).start()

        def start_one(offset, carry):
            slab_copy(which, offset).start()
            return carry

        lax.fori_loop(1, group, start_one, 0)

    def gather(which):
        parts = exchanges[which][1]

        def wait_one(offset, carry):
            origin = lax.rem(here + offset, group)
            pltpu.make_async_remote_copy(
                src_ref=parts.at[origin], dst_ref=parts.at[origin],
                send_sem=ts.at[which, offset], recv_sem=tr.at[which, origin],
                device_id=twin, device_id_type=MESH,
            ).wait_recv()
            return carry

        lax.fori_loop(1, group, wait_one, 0)
        self_copy(which).wait()
        return parts

    estat[...] = jnp.zeros_like(estat)
    dstat[...] = jnp.zeros_like(dstat)
    wide[...] = jnp.zeros_like(wide)

    def attend(half, slots, first=False):
        def body(head, carry):
            item = half * heads + head
            at = pl.ds(pl.multiple_of(head * HEAD_DIM, HEAD_DIM), HEAD_DIM)
            query = qb[half, :, at]
            parts = [scores_of(query, kb[slot, :, :, at].reshape(2 * rows, HEAD_DIM)) for slot in slots]
            new_top = functools.reduce(jnp.maximum, [jnp.max(part, axis=1, keepdims=True) for part in parts])
            if not first:
                new_top = jnp.maximum(new_top, top[item])
            mixed, summed = None, None
            for slot, part in zip(slots, parts):
                weights = jnp.exp2((part - new_top) * STEEP)
                one = jnp.sum(weights, axis=1, keepdims=True)
                two = jnp.dot(
                    weights.astype(jnp.bfloat16),
                    vb[slot, :, :, at].reshape(2 * rows, HEAD_DIM),
                    preferred_element_type=jnp.float32,
                )
                summed = one if summed is None else summed + one
                mixed = two if mixed is None else mixed + two
            if not first:
                shrink = jnp.exp2((top[item] - new_top) * STEEP)
                summed = summed + total[item] * shrink
                mixed = mixed + acc[item] * shrink
            top[item] = new_top
            total[item] = summed
            acc[item] = mixed
            return carry

        lax.fori_loop(0, heads, body, 0)

    def visit(slot):
        def body(head, carry):
            at = pl.ds(pl.multiple_of(head * HEAD_DIM, HEAD_DIM), HEAD_DIM)
            query = db[slot, :, :, at].reshape(2 * drows, HEAD_DIM)
            part = scores_of(query, ckb[:, :, at].reshape(2 * rows, HEAD_DIM))
            row_top = jnp.max(part, axis=1, keepdims=True)
            weights = jnp.exp2((part - row_top) * STEEP)
            summed = jnp.sum(weights, axis=1, keepdims=True)
            mixed = jnp.dot(
                weights.astype(jnp.bfloat16), cvb[:, :, at].reshape(2 * rows, HEAD_DIM),
                preferred_element_type=jnp.float32,
            )
            psend[slot, :, at] = mixed.astype(jnp.bfloat16)
            lane = lax.broadcasted_iota(jnp.int32, (2 * drows, HEAD_DIM), 1)
            held = dstat[0 : 2 * drows, :]
            held = jnp.where(lane == head, row_top, held)
            dstat[0 : 2 * drows, :] = jnp.where(lane == heads + head, summed, held)
            return carry

        lax.fori_loop(0, heads, body, 0)
        psend_stat[slot] = jnp.transpose(dstat[...])[0:8]
        if slot > 0:
            send(psend.at[slot], pback.at[slot], rs.at[slot], rr.at[slot], along(-slot))
            send(psend_stat.at[slot], pback_stat.at[slot], rts.at[slot], rtr.at[slot], along(-slot))
        else:
            pback[0] = psend[0]
            pback_stat[0] = psend_stat[0]

    def place(which, *targets):
        parts = gather(which)
        count = parts.shape[1]
        for source in range(group):
            for target in targets:
                target[source * count : (source + 1) * count, :] = parts[source]

    def hop(step):
        pair = (step,) if step == RING - step else (step, RING - step)
        for slot in pair:
            arrived(kb.at[slot, 0], kr.at[slot])
            pass_on(kb.at[slot, 0], slot, key_slot, ks, kr, KEY_RIGHT)
            send(kb.at[slot, 0], kb.at[slot, 1], kps.at[slot], kpr.at[slot], twin)
        for slot in pair:
            arrived(vb.at[slot, 0], vr.at[slot])
            pass_on(vb.at[slot, 0], slot, value_slot, vs, vr, VALUE_RIGHT)
            send(vb.at[slot, 0], vb.at[slot, 1], vps.at[slot], vpr.at[slot], twin)

    def query_hop(step):
        for slot in (step,) if step == RING - step else (step, RING - step):
            arrived(db.at[slot], dr.at[slot])
            pass_on(db.at[slot], slot, query_slot, ds, dr, KEY_RIGHT)

    def from_twin(*slots):
        for slot in slots:
            arrived(kb.at[slot, 1], kpr.at[slot])
            arrived(vb.at[slot, 1], vpr.at[slot])

    place(0, dq_ref, db.at[0, 0])
    send(dq_ref, db.at[0, 1], ms.at[0], mr.at[0], mirror)
    place(1, kb.at[0, 0])
    pass_on(kb.at[0, 0], 0, key_slot, ks, kr, KEY_RIGHT)
    send(kb.at[0, 0], kb.at[0, 1], kps.at[0], kpr.at[0], twin)
    arrived(db.at[0, 1], mr.at[0])
    pass_on(db.at[0], 0, query_slot, ds, dr, KEY_RIGHT)
    place(2, vb.at[0, 0])
    pass_on(vb.at[0, 0], 0, value_slot, vs, vr, VALUE_RIGHT)
    send(vb.at[0, 0], vb.at[0, 1], vps.at[0], vpr.at[0], twin)
    query_hop(1)
    hop(1)
    query_hop(2)
    place(3, qb.at[0])
    send(qb.at[0], qb.at[1], ms.at[1], mr.at[1], mirror)
    from_twin(0)
    attend(0, (0,), True)
    hop(2)
    query_hop(3)
    from_twin(1, 7)
    attend(0, (1, 7))
    place(4, ckb.at[0])
    send(ckb.at[0], ckb.at[1], ms.at[2], mr.at[2], twin)
    place(5, cvb.at[0])
    send(cvb.at[0], cvb.at[1], ms.at[3], mr.at[3], twin)
    hop(3)
    query_hop(4)
    from_twin(2, 6)
    attend(0, (2, 6))
    arrived(ckb.at[1], mr.at[2])
    arrived(cvb.at[1], mr.at[3])
    for slot in (4, 3, 5, 2, 6, 1, 7, 0):
        visit(slot)
    arrived(qb.at[1], mr.at[1])
    attend(1, (0,), True)
    attend(1, (1, 7))
    attend(1, (2, 6))
    from_twin(3, 5)
    attend(1, (3, 5))
    hop(4)
    from_twin(4)
    attend(1, (4,))

    lane = lax.broadcasted_iota(jnp.int32, (rows, HEAD_DIM), 1)
    held = jnp.zeros((rows, HEAD_DIM), jnp.float32)
    for head in range(heads):
        item = heads + head
        esend[:, head * HEAD_DIM : (head + 1) * HEAD_DIM] = acc[item].astype(jnp.bfloat16)
        held = jnp.where(lane == head, top[item], held)
        held = jnp.where(lane == heads + head, total[item], held)
    estat[0:rows, :] = held
    for chunk in range(2):
        esend_stat[chunk] = jnp.transpose(estat[chunk * 128 : (chunk + 1) * 128, :])[0:8]
    send(esend, eback, ms.at[4], mr.at[4], mirror)
    send(esend_stat, eback_stat, ms.at[5], mr.at[5], mirror)
    attend(0, (3, 5))
    attend(0, (4,))

    for slot in range(1, RING):
        arrived(pback.at[slot], rr.at[slot])
        arrived(pback_stat.at[slot], rtr.at[slot])
    stats = [pback_stat[slot] for slot in range(RING)]
    best = functools.reduce(jnp.maximum, [stat[0:heads] for stat in stats])
    joined = None
    for slot in range(RING):
        weight = jnp.exp2((stats[slot][0:heads] - best) * STEEP)
        wide[slot * 8 : slot * 8 + heads, :] = weight
        term = weight * stats[slot][heads : 2 * heads]
        joined = term if joined is None else joined + term
    zsend_stat[...] = jnp.zeros_like(zsend_stat)
    zsend_stat[0:heads, :] = best
    zsend_stat[heads : 2 * heads, :] = joined
    turned = jnp.transpose(wide[...])
    for head in range(heads):
        span = slice(head * HEAD_DIM, (head + 1) * HEAD_DIM)
        mixed = None
        for slot in range(RING):
            term = pback[slot, :, span].astype(jnp.float32) * turned[0 : 2 * drows, slot * 8 + head : slot * 8 + head + 1]
            mixed = term if mixed is None else mixed + term
        dmix[:, span] = mixed
        zsend[:, span] = mixed[drows:].astype(jnp.bfloat16)
    send(zsend, zback, ms.at[6], mr.at[6], mirror)
    send(zsend_stat, zback_stat, ms.at[7], mr.at[7], mirror)

    arrived(eback, mr.at[4])
    arrived(eback_stat, mr.at[5])
    wide[8:, :] = jnp.zeros((120, 128), jnp.float32)
    for chunk in range(2):
        wide[0:8, :] = eback_stat[chunk]
        estat[chunk * 128 : (chunk + 1) * 128, :] = jnp.transpose(wide[...])
    for head in range(heads):
        span = slice(head * HEAD_DIM, (head + 1) * HEAD_DIM)
        other_top = estat[0:rows, head : head + 1]
        other_total = estat[0:rows, heads + head : heads + head + 1]
        peak = jnp.maximum(top[head], other_top)
        mine = jnp.exp2((top[head] - peak) * STEEP)
        theirs = jnp.exp2((other_top - peak) * STEEP)
        whole = mine * acc[head] + theirs * eback[:, span].astype(jnp.float32)
        enc_ref[:, span] = (whole / (mine * total[head] + theirs * other_total)).astype(jnp.bfloat16)

    arrived(zback, mr.at[6])
    arrived(zback_stat, mr.at[7])
    wide[0:8, :] = zsend_stat[...]
    wide[8:16, :] = zback_stat[...]
    turned = jnp.transpose(wide[...])
    for head in range(heads):
        span = slice(head * HEAD_DIM, (head + 1) * HEAD_DIM)
        own_top = turned[0:drows, head : head + 1]
        own_total = turned[0:drows, heads + head : heads + head + 1]
        other_top = turned[drows : 2 * drows, 8 + head : 8 + head + 1]
        other_total = turned[drows : 2 * drows, 8 + heads + head : 8 + heads + head + 1]
        peak = jnp.maximum(own_top, other_top)
        mine = jnp.exp2((own_top - peak) * STEEP)
        theirs = jnp.exp2((other_top - peak) * STEEP)
        whole = mine * dmix[0:drows, span] + theirs * zback[:, span].astype(jnp.float32)
        dec_ref[:, span] = (whole / (mine * own_total + theirs * other_total)).astype(jnp.bfloat16)

    for copy in started:
        copy.wait_send()
    for which in range(6):

        def drain_one(offset, carry):
            slab_copy(which, offset).wait_send()
            return carry

        lax.fori_loop(1, group, drain_one, 0)


def attention(query, key, value, dec_query, cross_key, cross_value):
    group = lax.axis_size("tp")
    tokens, dtokens = query.shape[0], dec_query.shape[0]
    rows, drows, columns = group * tokens, group * dtokens, query.shape[1] // group
    heads = columns // HEAD_DIM
    bf16, f32 = jnp.bfloat16, jnp.float32
    vmem = pl.BlockSpec(memory_space=pltpu.VMEM)
    eight = pltpu.SemaphoreType.DMA((RING,))
    return pl.pallas_call(
        kernel,
        out_shape=(
            jax.ShapeDtypeStruct((rows, columns), bf16),
            jax.ShapeDtypeStruct((drows, columns), bf16),
        ),
        in_specs=[pl.BlockSpec(memory_space=pl.ANY)] * 6,
        out_specs=(vmem, vmem),
        scratch_shapes=[
            pltpu.VMEM((group, tokens, columns), bf16),
            pltpu.VMEM((group, tokens, columns), bf16),
            pltpu.VMEM((group, tokens, columns), bf16),
            pltpu.VMEM((group, dtokens, columns), bf16),
            pltpu.VMEM((group, tokens, columns), bf16),
            pltpu.VMEM((group, tokens, columns), bf16),
            pltpu.VMEM((drows, columns), bf16),
            pltpu.VMEM((2, rows, columns), bf16),
            pltpu.VMEM((RING, 2, rows, columns), bf16),
            pltpu.VMEM((RING, 2, rows, columns), bf16),
            pltpu.VMEM((RING, 2, drows, columns), bf16),
            pltpu.VMEM((2, rows, columns), bf16),
            pltpu.VMEM((2, rows, columns), bf16),
            pltpu.VMEM((2 * heads, rows, 1), f32),
            pltpu.VMEM((2 * heads, rows, 1), f32),
            pltpu.VMEM((2 * heads, rows, HEAD_DIM), f32),
            pltpu.VMEM((256, 128), f32),
            pltpu.VMEM((128, 128), f32),
            pltpu.VMEM((rows, columns), bf16),
            pltpu.VMEM((2, 8, 128), f32),
            pltpu.VMEM((rows, columns), bf16),
            pltpu.VMEM((2, 8, 128), f32),
            pltpu.VMEM((RING, 2 * drows, columns), bf16),
            pltpu.VMEM((RING, 8, 128), f32),
            pltpu.VMEM((RING, 2 * drows, columns), bf16),
            pltpu.VMEM((RING, 8, 128), f32),
            pltpu.VMEM((128, 128), f32),
            pltpu.VMEM((drows, columns), bf16),
            pltpu.VMEM((8, 128), f32),
            pltpu.VMEM((drows, columns), bf16),
            pltpu.VMEM((8, 128), f32),
            pltpu.VMEM((2 * drows, columns), f32),
        ]
        + [eight] * 16
        + [pltpu.SemaphoreType.DMA((6, group))] * 2
        + [pltpu.SemaphoreType.DMA((6,))],
        compiler_params=pltpu.CompilerParams(
            collective_id=0, has_side_effects=True, vmem_limit_bytes=67043328
        ),
    )(query, key, value, dec_query, cross_key, cross_value)


def shards(enc_query, enc_key, enc_value, dec_query, cross_key, cross_value):
    return attention(enc_query, enc_key, enc_value, dec_query, cross_key, cross_value)


def solution(mesh):
    in_specs = (P(("ctx", "tp"), None),) * 6
    out_specs = (P("ctx", "tp"), P("ctx", "tp"))
    return jax.shard_map(shards, mesh=mesh, in_specs=in_specs, out_specs=out_specs, check_vma=False)
```

```python
import functools

import jax
import jax.numpy as jnp
from jax import lax
from jax.experimental import pallas as pl
from jax.experimental.pallas import tpu as pltpu
from jax.sharding import PartitionSpec as P

HEAD_DIM = 128
RING = 8
LOG2E = 1.4426950408889634
STEEP = HEAD_DIM ** (-0.5) * LOG2E
MESH = pl.DeviceIdType.MESH
KEY_RIGHT = (1, 2, 3, 4)
VALUE_RIGHT = (1, 2, 3)


def scores_of(query, key):
    return lax.dot_general(query, key, (((1,), (1,)), ((), ())), preferred_element_type=jnp.float32)


def kernel(
    q_arg, k_arg, v_arg, dq_arg, ck_arg, cv_arg, enc_ref, dec_ref,
    q_parts, k_parts, v_parts, dq_parts, ck_parts, cv_parts,
    dq_ref, qb, kb, vb, db, ckb, cvb, top, total, acc, estat, dstat,
    esend, esend_stat, eback, eback_stat, psend, psend_stat, pback, pback_stat,
    wide, zsend, zsend_stat, zback, zback_stat, dmix,
    ks, kr, vs, vr, ds, dr, kps, kpr, vps, vpr, rs, rr, rts, rtr, ms, mr, ts, tr, self_sems,
):
    rows, columns = enc_ref.shape
    drows = dq_ref.shape[0]
    tokens = q_arg.shape[0]
    dtokens = dq_arg.shape[0]
    group = q_parts.shape[0]
    here = lax.axis_index("tp")
    heads = columns // HEAD_DIM
    me = lax.axis_index("ctx")
    plane, y, core = me // (2 * RING), (me // 2) % RING, me % 2

    def along(offset):
        return {"ctx": plane * (2 * RING) + lax.rem(y + offset + RING, RING) * 2 + core}

    twin = {"ctx": plane * (2 * RING) + y * 2 + (1 - core)}
    mirror = {"ctx": (1 - plane) * (2 * RING) + y * 2 + core}

    barrier = pltpu.get_barrier_semaphore()
    for peer in [along(offset) for offset in range(1, RING)] + [twin, mirror]:
        pl.semaphore_signal(barrier, inc=1, device_id=peer, device_id_type=MESH)
    for offset in range(1, group):
        pl.semaphore_signal(
            barrier, inc=1, device_id={"tp": lax.rem(here + offset, group)}, device_id_type=MESH
        )
    pl.semaphore_wait(barrier, RING + group)

    started = []

    def send(source, target, send_sem, recv_sem, device):
        copy = pltpu.make_async_remote_copy(
            src_ref=source, dst_ref=target, send_sem=send_sem, recv_sem=recv_sem,
            device_id=device, device_id_type=MESH,
        )
        copy.start()
        started.append(copy)

    def arrived(target, recv_sem):
        pltpu.make_async_remote_copy(
            src_ref=target, dst_ref=target, send_sem=recv_sem, recv_sem=recv_sem,
            device_id=twin, device_id_type=MESH,
        ).wait_recv()

    def onward(source, slot, buffer, send_sems, recv_sems, right):
        after, before = (slot + 1) % RING, (slot - 1) % RING
        if after in right:
            send(source, buffer(after), send_sems.at[after], recv_sems.at[after], along(1))
        if before not in right and before != 0:
            send(source, buffer(before), send_sems.at[before], recv_sems.at[before], along(-1))

    def pass_on(source, slot, buffer, send_sems, recv_sems, right):
        if slot == 0:
            onward(source, 0, buffer, send_sems, recv_sems, right)
        elif slot in right:
            if slot + 1 in right:
                send(source, buffer(slot + 1), send_sems.at[slot + 1], recv_sems.at[slot + 1], along(1))
        elif slot - 1 not in right and slot - 1 != 0:
            send(source, buffer(slot - 1), send_sems.at[slot - 1], recv_sems.at[slot - 1], along(-1))

    def key_slot(slot):
        return kb.at[slot, 0]

    def value_slot(slot):
        return vb.at[slot, 0]

    def query_slot(slot):
        return db.at[slot]

    exchanges = (
        (dq_arg, dq_parts), (k_arg, k_parts), (v_arg, v_parts),
        (q_arg, q_parts), (ck_arg, ck_parts), (cv_arg, cv_parts),
    )

    def slab(which, peer):
        argument, parts = exchanges[which]
        return argument.at[:, pl.ds(pl.multiple_of(peer * columns, 128), columns)]

    def slab_copy(which, offset):
        peer = lax.rem(here + offset, group)
        return pltpu.make_async_remote_copy(
            src_ref=slab(which, peer), dst_ref=exchanges[which][1].at[here],
            send_sem=ts.at[which, offset], recv_sem=tr.at[which, here],
            device_id={"tp": peer}, device_id_type=MESH,
        )

    def self_copy(which):
        return pltpu.make_async_copy(slab(which, here), exchanges[which][1].at[here], self_sems.at[which])

    for which in range(6):
        self_copy(which).start()

        def start_one(offset, carry):
            slab_copy(which, offset).start()
            return carry

        lax.fori_loop(1, group, start_one, 0)

    def gather(which):
        parts = exchanges[which][1]

        def wait_one(offset, carry):
            origin = lax.rem(here + offset, group)
            pltpu.make_async_remote_copy(
                src_ref=parts.at[origin], dst_ref=parts.at[origin],
                send_sem=ts.at[which, offset], recv_sem=tr.at[which, origin],
                device_id=twin, device_id_type=MESH,
            ).wait_recv()
            return carry

        lax.fori_loop(1, group, wait_one, 0)
        self_copy(which).wait()
        return parts

    estat[...] = jnp.zeros_like(estat)
    dstat[...] = jnp.zeros_like(dstat)
    wide[...] = jnp.zeros_like(wide)

    def attend(span, slots, first=False):
        count = span.stop - span.start

        def body(head, carry):
            at = pl.ds(pl.multiple_of(head * HEAD_DIM, HEAD_DIM), HEAD_DIM)
            query = qb[:, :, at].reshape(2 * rows, HEAD_DIM)[span]
            parts = [scores_of(query, kb[slot, :, :, at].reshape(2 * rows, HEAD_DIM)) for slot in slots]
            new_top = functools.reduce(jnp.maximum, [jnp.max(part, axis=1, keepdims=True) for part in parts])
            if not first:
                new_top = jnp.maximum(new_top, top[head, span])
            mixed, summed = None, None
            for slot, part in zip(slots, parts):
                weights = jnp.exp2((part - new_top) * STEEP)
                one = jnp.sum(weights, axis=1, keepdims=True)
                two = jnp.dot(
                    weights.astype(jnp.bfloat16),
                    vb[slot, :, :, at].reshape(2 * rows, HEAD_DIM),
                    preferred_element_type=jnp.float32,
                )
                summed = one if summed is None else summed + one
                mixed = two if mixed is None else mixed + two
            if not first:
                shrink = jnp.exp2((top[head, span] - new_top) * STEEP)
                summed = summed + total[head, span] * shrink
                mixed = mixed + acc[head, span] * shrink
            top[head, span] = new_top
            total[head, span] = summed
            acc[head, span] = mixed
            return carry

        lax.fori_loop(0, heads, body, 0)

    own_rows, mirror_rows, both = slice(0, rows), slice(rows, 2 * rows), slice(0, 2 * rows)

    def visit_all():
        some = RING // 2

        def body(item, carry):
            start, head = (item // heads) * some, item % heads
            at = pl.ds(pl.multiple_of(head * HEAD_DIM, HEAD_DIM), HEAD_DIM)
            query = db[pl.ds(start, some), :, :, at].reshape(some * 2 * drows, HEAD_DIM)
            part = scores_of(query, ckb[:, :, at].reshape(2 * rows, HEAD_DIM))
            row_top = jnp.max(part, axis=1, keepdims=True)
            weights = jnp.exp2((part - row_top) * STEEP)
            summed = jnp.sum(weights, axis=1, keepdims=True)
            mixed = jnp.dot(
                weights.astype(jnp.bfloat16), cvb[:, :, at].reshape(2 * rows, HEAD_DIM),
                preferred_element_type=jnp.float32,
            )
            psend[pl.ds(start, some), :, at] = mixed.astype(jnp.bfloat16).reshape(some, 2 * drows, HEAD_DIM)
            lane = lax.broadcasted_iota(jnp.int32, (some, 2 * drows, HEAD_DIM), 2)
            held = dstat[pl.ds(start, some), 0 : 2 * drows, :]
            held = jnp.where(lane == head, row_top.reshape(some, 2 * drows, 1), held)
            held = jnp.where(lane == heads + head, summed.reshape(some, 2 * drows, 1), held)
            dstat[pl.ds(start, some), 0 : 2 * drows, :] = held
            return carry

        lax.fori_loop(0, 2 * heads, body, 0)
        for slot in (4, 3, 5, 2, 6, 1, 7):
            psend_stat[slot] = jnp.transpose(dstat[slot])[0:8]
            send(psend.at[slot], pback.at[slot], rs.at[slot], rr.at[slot], along(-slot))
            send(psend_stat.at[slot], pback_stat.at[slot], rts.at[slot], rtr.at[slot], along(-slot))
        pback[0] = psend[0]
        pback_stat[0] = jnp.transpose(dstat[0])[0:8]

    def place(which, *targets):
        parts = gather(which)
        count = parts.shape[1]
        for source in range(group):
            for target in targets:
                target[source * count : (source + 1) * count, :] = parts[source]

    def hop(step):
        pair = (step,) if step == RING - step else (step, RING - step)
        for slot in pair:
            arrived(kb.at[slot, 0], kr.at[slot])
            pass_on(kb.at[slot, 0], slot, key_slot, ks, kr, KEY_RIGHT)
            send(kb.at[slot, 0], kb.at[slot, 1], kps.at[slot], kpr.at[slot], twin)
        for slot in pair:
            arrived(vb.at[slot, 0], vr.at[slot])
            pass_on(vb.at[slot, 0], slot, value_slot, vs, vr, VALUE_RIGHT)
            send(vb.at[slot, 0], vb.at[slot, 1], vps.at[slot], vpr.at[slot], twin)

    def query_hop(step):
        for slot in (step,) if step == RING - step else (step, RING - step):
            arrived(db.at[slot], dr.at[slot])
            pass_on(db.at[slot], slot, query_slot, ds, dr, KEY_RIGHT)

    def from_twin(*slots):
        for slot in slots:
            arrived(kb.at[slot, 1], kpr.at[slot])
            arrived(vb.at[slot, 1], vpr.at[slot])

    place(0, dq_ref, db.at[0, 0])
    send(dq_ref, db.at[0, 1], ms.at[0], mr.at[0], mirror)
    place(1, kb.at[0, 0])
    pass_on(kb.at[0, 0], 0, key_slot, ks, kr, KEY_RIGHT)
    send(kb.at[0, 0], kb.at[0, 1], kps.at[0], kpr.at[0], twin)
    arrived(db.at[0, 1], mr.at[0])
    pass_on(db.at[0], 0, query_slot, ds, dr, KEY_RIGHT)
    place(2, vb.at[0, 0])
    pass_on(vb.at[0, 0], 0, value_slot, vs, vr, VALUE_RIGHT)
    send(vb.at[0, 0], vb.at[0, 1], vps.at[0], vpr.at[0], twin)
    query_hop(1)
    hop(1)
    query_hop(2)
    place(3, qb.at[0])
    send(qb.at[0], qb.at[1], ms.at[1], mr.at[1], mirror)
    hop(2)
    query_hop(3)
    place(4, ckb.at[0])
    send(ckb.at[0], ckb.at[1], ms.at[2], mr.at[2], twin)
    place(5, cvb.at[0])
    send(cvb.at[0], cvb.at[1], ms.at[3], mr.at[3], twin)
    hop(3)
    query_hop(4)
    arrived(ckb.at[1], mr.at[2])
    arrived(cvb.at[1], mr.at[3])
    visit_all()
    arrived(qb.at[1], mr.at[1])
    from_twin(0)
    attend(both, (0,), True)
    from_twin(1, 7)
    attend(both, (1, 7))
    from_twin(2, 6)
    attend(both, (2, 6))
    from_twin(3, 5)
    attend(both, (3, 5))
    hop(4)
    from_twin(4)
    attend(mirror_rows, (4,))

    lane = lax.broadcasted_iota(jnp.int32, (rows, HEAD_DIM), 1)
    held = jnp.zeros((rows, HEAD_DIM), jnp.float32)
    for head in range(heads):
        esend[:, head * HEAD_DIM : (head + 1) * HEAD_DIM] = acc[head, mirror_rows].astype(jnp.bfloat16)
        held = jnp.where(lane == head, top[head, mirror_rows], held)
        held = jnp.where(lane == heads + head, total[head, mirror_rows], held)
    estat[0:rows, :] = held
    for chunk in range(2):
        esend_stat[chunk] = jnp.transpose(estat[chunk * 128 : (chunk + 1) * 128, :])[0:8]
    send(esend, eback, ms.at[4], mr.at[4], mirror)
    send(esend_stat, eback_stat, ms.at[5], mr.at[5], mirror)
    attend(own_rows, (4,))

    for slot in range(1, RING):
        arrived(pback.at[slot], rr.at[slot])
        arrived(pback_stat.at[slot], rtr.at[slot])
    stats = [pback_stat[slot] for slot in range(RING)]
    best = functools.reduce(jnp.maximum, [stat[0:heads] for stat in stats])
    joined = None
    for slot in range(RING):
        weight = jnp.exp2((stats[slot][0:heads] - best) * STEEP)
        wide[slot * 8 : slot * 8 + heads, :] = weight
        term = weight * stats[slot][heads : 2 * heads]
        joined = term if joined is None else joined + term
    zsend_stat[...] = jnp.zeros_like(zsend_stat)
    zsend_stat[0:heads, :] = best
    zsend_stat[heads : 2 * heads, :] = joined
    turned = jnp.transpose(wide[...])
    for head in range(heads):
        span = slice(head * HEAD_DIM, (head + 1) * HEAD_DIM)
        mixed = None
        for slot in range(RING):
            term = pback[slot, :, span].astype(jnp.float32) * turned[0 : 2 * drows, slot * 8 + head : slot * 8 + head + 1]
            mixed = term if mixed is None else mixed + term
        dmix[:, span] = mixed
        zsend[:, span] = mixed[drows:].astype(jnp.bfloat16)
    send(zsend, zback, ms.at[6], mr.at[6], mirror)
    send(zsend_stat, zback_stat, ms.at[7], mr.at[7], mirror)

    arrived(eback, mr.at[4])
    arrived(eback_stat, mr.at[5])
    wide[8:, :] = jnp.zeros((120, 128), jnp.float32)
    for chunk in range(2):
        wide[0:8, :] = eback_stat[chunk]
        estat[chunk * 128 : (chunk + 1) * 128, :] = jnp.transpose(wide[...])
    for head in range(heads):
        span = slice(head * HEAD_DIM, (head + 1) * HEAD_DIM)
        other_top = estat[0:rows, head : head + 1]
        other_total = estat[0:rows, heads + head : heads + head + 1]
        peak = jnp.maximum(top[head, own_rows], other_top)
        mine = jnp.exp2((top[head, own_rows] - peak) * STEEP)
        theirs = jnp.exp2((other_top - peak) * STEEP)
        whole = mine * acc[head, own_rows] + theirs * eback[:, span].astype(jnp.float32)
        enc_ref[:, span] = (whole / (mine * total[head, own_rows] + theirs * other_total)).astype(jnp.bfloat16)

    arrived(zback, mr.at[6])
    arrived(zback_stat, mr.at[7])
    wide[0:8, :] = zsend_stat[...]
    wide[8:16, :] = zback_stat[...]
    turned = jnp.transpose(wide[...])
    for head in range(heads):
        span = slice(head * HEAD_DIM, (head + 1) * HEAD_DIM)
        own_top = turned[0:drows, head : head + 1]
        own_total = turned[0:drows, heads + head : heads + head + 1]
        other_top = turned[drows : 2 * drows, 8 + head : 8 + head + 1]
        other_total = turned[drows : 2 * drows, 8 + heads + head : 8 + heads + head + 1]
        peak = jnp.maximum(own_top, other_top)
        mine = jnp.exp2((own_top - peak) * STEEP)
        theirs = jnp.exp2((other_top - peak) * STEEP)
        whole = mine * dmix[0:drows, span] + theirs * zback[:, span].astype(jnp.float32)
        dec_ref[:, span] = (whole / (mine * own_total + theirs * other_total)).astype(jnp.bfloat16)

    for copy in started:
        copy.wait_send()
    for which in range(6):

        def drain_one(offset, carry):
            slab_copy(which, offset).wait_send()
            return carry

        lax.fori_loop(1, group, drain_one, 0)


def attention(query, key, value, dec_query, cross_key, cross_value):
    group = lax.axis_size("tp")
    tokens, dtokens = query.shape[0], dec_query.shape[0]
    rows, drows, columns = group * tokens, group * dtokens, query.shape[1] // group
    heads = columns // HEAD_DIM
    bf16, f32 = jnp.bfloat16, jnp.float32
    vmem = pl.BlockSpec(memory_space=pltpu.VMEM)
    eight = pltpu.SemaphoreType.DMA((RING,))
    return pl.pallas_call(
        kernel,
        out_shape=(
            jax.ShapeDtypeStruct((rows, columns), bf16),
            jax.ShapeDtypeStruct((drows, columns), bf16),
        ),
        in_specs=[pl.BlockSpec(memory_space=pl.ANY)] * 6,
        out_specs=(vmem, vmem),
        scratch_shapes=[
            pltpu.VMEM((group, tokens, columns), bf16),
            pltpu.VMEM((group, tokens, columns), bf16),
            pltpu.VMEM((group, tokens, columns), bf16),
            pltpu.VMEM((group, dtokens, columns), bf16),
            pltpu.VMEM((group, tokens, columns), bf16),
            pltpu.VMEM((group, tokens, columns), bf16),
            pltpu.VMEM((drows, columns), bf16),
            pltpu.VMEM((2, rows, columns), bf16),
            pltpu.VMEM((RING, 2, rows, columns), bf16),
            pltpu.VMEM((RING, 2, rows, columns), bf16),
            pltpu.VMEM((RING, 2, drows, columns), bf16),
            pltpu.VMEM((2, rows, columns), bf16),
            pltpu.VMEM((2, rows, columns), bf16),
            pltpu.VMEM((heads, 2 * rows, 1), f32),
            pltpu.VMEM((heads, 2 * rows, 1), f32),
            pltpu.VMEM((heads, 2 * rows, HEAD_DIM), f32),
            pltpu.VMEM((256, 128), f32),
            pltpu.VMEM((RING, 128, 128), f32),
            pltpu.VMEM((rows, columns), bf16),
            pltpu.VMEM((2, 8, 128), f32),
            pltpu.VMEM((rows, columns), bf16),
            pltpu.VMEM((2, 8, 128), f32),
            pltpu.VMEM((RING, 2 * drows, columns), bf16),
            pltpu.VMEM((RING, 8, 128), f32),
            pltpu.VMEM((RING, 2 * drows, columns), bf16),
            pltpu.VMEM((RING, 8, 128), f32),
            pltpu.VMEM((128, 128), f32),
            pltpu.VMEM((drows, columns), bf16),
            pltpu.VMEM((8, 128), f32),
            pltpu.VMEM((drows, columns), bf16),
            pltpu.VMEM((8, 128), f32),
            pltpu.VMEM((2 * drows, columns), f32),
        ]
        + [eight] * 16
        + [pltpu.SemaphoreType.DMA((6, group))] * 2
        + [pltpu.SemaphoreType.DMA((6,))],
        compiler_params=pltpu.CompilerParams(
            collective_id=0, has_side_effects=True, vmem_limit_bytes=67043328
        ),
    )(query, key, value, dec_query, cross_key, cross_value)


def shards(enc_query, enc_key, enc_value, dec_query, cross_key, cross_value):
    return attention(enc_query, enc_key, enc_value, dec_query, cross_key, cross_value)


def solution(mesh):
    in_specs = (P(("ctx", "tp"), None),) * 6
    out_specs = (P("ctx", "tp"), P("ctx", "tp"))
    return jax.shard_map(shards, mesh=mesh, in_specs=in_specs, out_specs=out_specs, check_vma=False)
```

```python
import functools

import jax
import jax.numpy as jnp
from jax import lax
from jax.experimental import pallas as pl
from jax.experimental.pallas import tpu as pltpu
from jax.sharding import PartitionSpec as P

HEAD_DIM = 128
RING = 8
LOG2E = 1.4426950408889634
STEEP = HEAD_DIM ** (-0.5) * LOG2E
MESH = pl.DeviceIdType.MESH
KEY_RIGHT = (1, 2, 3, 4)
VALUE_RIGHT = (1, 2, 3)


def scores_of(query, key):
    return lax.dot_general(query, key, (((1,), (1,)), ((), ())), preferred_element_type=jnp.float32)


def kernel(
    q_arg, k_arg, v_arg, dq_arg, ck_arg, cv_arg, enc_ref, dec_ref,
    q_parts, k_parts, v_parts, dq_parts, ck_parts, cv_parts,
    dq_ref, qb, kb, vb, db, ckb, cvb, top, total, acc, estat, dstat,
    esend, esend_stat, eback, eback_stat, psend, psend_stat, pback, pback_stat,
    wide, zsend, zsend_stat, zback, zback_stat, dmix,
    ks, kr, vs, vr, ds, dr, kps, kpr, vps, vpr, rs, rr, rts, rtr, ms, mr, ts, tr, self_sems,
):
    rows, columns = enc_ref.shape
    drows = dq_ref.shape[0]
    tokens = q_arg.shape[0]
    dtokens = dq_arg.shape[0]
    group = q_parts.shape[0]
    here = lax.axis_index("tp")
    heads = columns // HEAD_DIM
    me = lax.axis_index("ctx")
    plane, y, core = me // (2 * RING), (me // 2) % RING, me % 2

    def along(offset):
        return {"ctx": plane * (2 * RING) + lax.rem(y + offset + RING, RING) * 2 + core}

    twin = {"ctx": plane * (2 * RING) + y * 2 + (1 - core)}
    mirror = {"ctx": (1 - plane) * (2 * RING) + y * 2 + core}

    barrier = pltpu.get_barrier_semaphore()
    for peer in [along(offset) for offset in range(1, RING)] + [twin, mirror]:
        pl.semaphore_signal(barrier, inc=1, device_id=peer, device_id_type=MESH)
    for offset in range(1, group):
        pl.semaphore_signal(
            barrier, inc=1, device_id={"tp": lax.rem(here + offset, group)}, device_id_type=MESH
        )
    pl.semaphore_wait(barrier, RING + group)

    started = []

    def send(source, target, send_sem, recv_sem, device):
        copy = pltpu.make_async_remote_copy(
            src_ref=source, dst_ref=target, send_sem=send_sem, recv_sem=recv_sem,
            device_id=device, device_id_type=MESH,
        )
        copy.start()
        started.append(copy)

    def arrived(target, recv_sem):
        pltpu.make_async_remote_copy(
            src_ref=target, dst_ref=target, send_sem=recv_sem, recv_sem=recv_sem,
            device_id=twin, device_id_type=MESH,
        ).wait_recv()

    def onward(source, slot, buffer, send_sems, recv_sems, right):
        after, before = (slot + 1) % RING, (slot - 1) % RING
        if after in right:
            send(source, buffer(after), send_sems.at[after], recv_sems.at[after], along(1))
        if before not in right and before != 0:
            send(source, buffer(before), send_sems.at[before], recv_sems.at[before], along(-1))

    def pass_on(source, slot, buffer, send_sems, recv_sems, right):
        if slot == 0:
            onward(source, 0, buffer, send_sems, recv_sems, right)
        elif slot in right:
            if slot + 1 in right:
                send(source, buffer(slot + 1), send_sems.at[slot + 1], recv_sems.at[slot + 1], along(1))
        elif slot - 1 not in right and slot - 1 != 0:
            send(source, buffer(slot - 1), send_sems.at[slot - 1], recv_sems.at[slot - 1], along(-1))

    def key_slot(slot):
        return kb.at[slot, 0]

    def value_slot(slot):
        return vb.at[slot, 0]

    def query_slot(slot):
        return db.at[slot]

    exchanges = (
        (dq_arg, dq_parts), (k_arg, k_parts), (v_arg, v_parts),
        (q_arg, q_parts), (ck_arg, ck_parts), (cv_arg, cv_parts),
    )

    def slab(which, peer):
        argument, parts = exchanges[which]
        return argument.at[:, pl.ds(pl.multiple_of(peer * columns, 128), columns)]

    def slab_copy(which, offset):
        peer = lax.rem(here + offset, group)
        return pltpu.make_async_remote_copy(
            src_ref=slab(which, peer), dst_ref=exchanges[which][1].at[here],
            send_sem=ts.at[which, offset], recv_sem=tr.at[which, here],
            device_id={"tp": peer}, device_id_type=MESH,
        )

    def self_copy(which):
        return pltpu.make_async_copy(slab(which, here), exchanges[which][1].at[here], self_sems.at[which])

    for which in range(6):
        self_copy(which).start()

        def start_one(offset, carry):
            slab_copy(which, offset).start()
            return carry

        lax.fori_loop(1, group, start_one, 0)

    def gather(which):
        parts = exchanges[which][1]

        def wait_one(offset, carry):
            origin = lax.rem(here + offset, group)
            pltpu.make_async_remote_copy(
                src_ref=parts.at[origin], dst_ref=parts.at[origin],
                send_sem=ts.at[which, offset], recv_sem=tr.at[which, origin],
                device_id=twin, device_id_type=MESH,
            ).wait_recv()
            return carry

        lax.fori_loop(1, group, wait_one, 0)
        self_copy(which).wait()
        return parts

    estat[...] = jnp.zeros_like(estat)
    dstat[...] = jnp.zeros_like(dstat)
    wide[...] = jnp.zeros_like(wide)

    def attend(span, slots, first=False):
        count = span.stop - span.start

        def body(head, carry):
            at = pl.ds(pl.multiple_of(head * HEAD_DIM, HEAD_DIM), HEAD_DIM)
            query = qb[:, :, at].reshape(2 * rows, HEAD_DIM)[span]
            parts = [scores_of(query, kb[slot, :, :, at].reshape(2 * rows, HEAD_DIM)) for slot in slots]
            new_top = functools.reduce(jnp.maximum, [jnp.max(part, axis=1, keepdims=True) for part in parts])
            if not first:
                new_top = jnp.maximum(new_top, top[head, span])
            mixed, summed = None, None
            for slot, part in zip(slots, parts):
                weights = jnp.exp2((part - new_top) * STEEP)
                one = jnp.sum(weights, axis=1, keepdims=True)
                two = jnp.dot(
                    weights.astype(jnp.bfloat16),
                    vb[slot, :, :, at].reshape(2 * rows, HEAD_DIM),
                    preferred_element_type=jnp.float32,
                )
                summed = one if summed is None else summed + one
                mixed = two if mixed is None else mixed + two
            if not first:
                shrink = jnp.exp2((top[head, span] - new_top) * STEEP)
                summed = summed + total[head, span] * shrink
                mixed = mixed + acc[head, span] * shrink
            top[head, span] = new_top
            total[head, span] = summed
            acc[head, span] = mixed
            return carry

        lax.fori_loop(0, heads, body, 0)

    own_rows, mirror_rows, both = slice(0, rows), slice(rows, 2 * rows), slice(0, 2 * rows)

    def visit_all():
        some = RING // 2

        def body(item, carry):
            start, head = (item // heads) * some, item % heads
            at = pl.ds(pl.multiple_of(head * HEAD_DIM, HEAD_DIM), HEAD_DIM)
            query = db[pl.ds(start, some), :, :, at].reshape(some * 2 * drows, HEAD_DIM)
            part = scores_of(query, ckb[:, :, at].reshape(2 * rows, HEAD_DIM))
            row_top = jnp.max(part, axis=1, keepdims=True)
            weights = jnp.exp2((part - row_top) * STEEP)
            summed = jnp.sum(weights, axis=1, keepdims=True)
            mixed = jnp.dot(
                weights.astype(jnp.bfloat16), cvb[:, :, at].reshape(2 * rows, HEAD_DIM),
                preferred_element_type=jnp.float32,
            )
            psend[pl.ds(start, some), :, at] = mixed.astype(jnp.bfloat16).reshape(some, 2 * drows, HEAD_DIM)
            lane = lax.broadcasted_iota(jnp.int32, (some, 2 * drows, HEAD_DIM), 2)
            held = dstat[pl.ds(start, some), 0 : 2 * drows, :]
            held = jnp.where(lane == head, row_top.reshape(some, 2 * drows, 1), held)
            held = jnp.where(lane == heads + head, summed.reshape(some, 2 * drows, 1), held)
            dstat[pl.ds(start, some), 0 : 2 * drows, :] = held
            return carry

        lax.fori_loop(0, 2 * heads, body, 0)
        for slot in range(1, RING):
            psend_stat[slot] = jnp.transpose(dstat[slot])[0:8]
        pback[0] = psend[0]
        pback_stat[0] = jnp.transpose(dstat[0])[0:8]

    def give_back():
        for slot in (4, 3, 5, 2, 6, 1, 7):
            send(psend.at[slot], pback.at[slot], rs.at[slot], rr.at[slot], along(-slot))
            send(psend_stat.at[slot], pback_stat.at[slot], rts.at[slot], rtr.at[slot], along(-slot))

    def place(which, *targets):
        parts = gather(which)
        count = parts.shape[1]
        for source in range(group):
            for target in targets:
                target[source * count : (source + 1) * count, :] = parts[source]

    def hop(step):
        pair = (step,) if step == RING - step else (step, RING - step)
        for slot in pair:
            arrived(kb.at[slot, 0], kr.at[slot])
            pass_on(kb.at[slot, 0], slot, key_slot, ks, kr, KEY_RIGHT)
            send(kb.at[slot, 0], kb.at[slot, 1], kps.at[slot], kpr.at[slot], twin)
        for slot in pair:
            arrived(vb.at[slot, 0], vr.at[slot])
            pass_on(vb.at[slot, 0], slot, value_slot, vs, vr, VALUE_RIGHT)
            send(vb.at[slot, 0], vb.at[slot, 1], vps.at[slot], vpr.at[slot], twin)

    def query_hop(step):
        for slot in (step,) if step == RING - step else (step, RING - step):
            arrived(db.at[slot], dr.at[slot])
            pass_on(db.at[slot], slot, query_slot, ds, dr, KEY_RIGHT)

    def from_twin(*slots):
        for slot in slots:
            arrived(kb.at[slot, 1], kpr.at[slot])
            arrived(vb.at[slot, 1], vpr.at[slot])

    place(0, dq_ref, db.at[0, 0])
    send(dq_ref, db.at[0, 1], ms.at[0], mr.at[0], mirror)
    place(1, kb.at[0, 0])
    pass_on(kb.at[0, 0], 0, key_slot, ks, kr, KEY_RIGHT)
    send(kb.at[0, 0], kb.at[0, 1], kps.at[0], kpr.at[0], twin)
    arrived(db.at[0, 1], mr.at[0])
    pass_on(db.at[0], 0, query_slot, ds, dr, KEY_RIGHT)
    place(2, vb.at[0, 0])
    pass_on(vb.at[0, 0], 0, value_slot, vs, vr, VALUE_RIGHT)
    send(vb.at[0, 0], vb.at[0, 1], vps.at[0], vpr.at[0], twin)
    query_hop(1)
    hop(1)
    query_hop(2)
    place(3, qb.at[0])
    send(qb.at[0], qb.at[1], ms.at[1], mr.at[1], mirror)
    hop(2)
    query_hop(3)
    place(4, ckb.at[0])
    send(ckb.at[0], ckb.at[1], ms.at[2], mr.at[2], twin)
    place(5, cvb.at[0])
    send(cvb.at[0], cvb.at[1], ms.at[3], mr.at[3], twin)
    hop(3)
    query_hop(4)
    arrived(ckb.at[1], mr.at[2])
    arrived(cvb.at[1], mr.at[3])
    visit_all()
    arrived(qb.at[1], mr.at[1])
    from_twin(0)
    attend(both, (0,), True)
    from_twin(1, 7)
    attend(both, (1, 7))
    from_twin(2, 6)
    attend(both, (2, 6))
    from_twin(3, 5)
    attend(both, (3, 5))
    hop(4)
    give_back()
    from_twin(4)
    attend(mirror_rows, (4,))

    lane = lax.broadcasted_iota(jnp.int32, (rows, HEAD_DIM), 1)
    held = jnp.zeros((rows, HEAD_DIM), jnp.float32)
    for head in range(heads):
        esend[:, head * HEAD_DIM : (head + 1) * HEAD_DIM] = acc[head, mirror_rows].astype(jnp.bfloat16)
        held = jnp.where(lane == head, top[head, mirror_rows], held)
        held = jnp.where(lane == heads + head, total[head, mirror_rows], held)
    estat[0:rows, :] = held
    for chunk in range(2):
        esend_stat[chunk] = jnp.transpose(estat[chunk * 128 : (chunk + 1) * 128, :])[0:8]
    send(esend, eback, ms.at[4], mr.at[4], mirror)
    send(esend_stat, eback_stat, ms.at[5], mr.at[5], mirror)
    attend(own_rows, (4,))

    for slot in range(1, RING):
        arrived(pback.at[slot], rr.at[slot])
        arrived(pback_stat.at[slot], rtr.at[slot])
    stats = [pback_stat[slot] for slot in range(RING)]
    best = functools.reduce(jnp.maximum, [stat[0:heads] for stat in stats])
    joined = None
    for slot in range(RING):
        weight = jnp.exp2((stats[slot][0:heads] - best) * STEEP)
        wide[slot * 8 : slot * 8 + heads, :] = weight
        term = weight * stats[slot][heads : 2 * heads]
        joined = term if joined is None else joined + term
    zsend_stat[...] = jnp.zeros_like(zsend_stat)
    zsend_stat[0:heads, :] = best
    zsend_stat[heads : 2 * heads, :] = joined
    turned = jnp.transpose(wide[...])
    for head in range(heads):
        span = slice(head * HEAD_DIM, (head + 1) * HEAD_DIM)
        mixed = None
        for slot in range(RING):
            term = pback[slot, :, span].astype(jnp.float32) * turned[0 : 2 * drows, slot * 8 + head : slot * 8 + head + 1]
            mixed = term if mixed is None else mixed + term
        dmix[:, span] = mixed
        zsend[:, span] = mixed[drows:].astype(jnp.bfloat16)
    send(zsend, zback, ms.at[6], mr.at[6], mirror)
    send(zsend_stat, zback_stat, ms.at[7], mr.at[7], mirror)

    arrived(eback, mr.at[4])
    arrived(eback_stat, mr.at[5])
    wide[8:, :] = jnp.zeros((120, 128), jnp.float32)
    for chunk in range(2):
        wide[0:8, :] = eback_stat[chunk]
        estat[chunk * 128 : (chunk + 1) * 128, :] = jnp.transpose(wide[...])
    for head in range(heads):
        span = slice(head * HEAD_DIM, (head + 1) * HEAD_DIM)
        other_top = estat[0:rows, head : head + 1]
        other_total = estat[0:rows, heads + head : heads + head + 1]
        peak = jnp.maximum(top[head, own_rows], other_top)
        mine = jnp.exp2((top[head, own_rows] - peak) * STEEP)
        theirs = jnp.exp2((other_top - peak) * STEEP)
        whole = mine * acc[head, own_rows] + theirs * eback[:, span].astype(jnp.float32)
        enc_ref[:, span] = (whole / (mine * total[head, own_rows] + theirs * other_total)).astype(jnp.bfloat16)

    arrived(zback, mr.at[6])
    arrived(zback_stat, mr.at[7])
    wide[0:8, :] = zsend_stat[...]
    wide[8:16, :] = zback_stat[...]
    turned = jnp.transpose(wide[...])
    for head in range(heads):
        span = slice(head * HEAD_DIM, (head + 1) * HEAD_DIM)
        own_top = turned[0:drows, head : head + 1]
        own_total = turned[0:drows, heads + head : heads + head + 1]
        other_top = turned[drows : 2 * drows, 8 + head : 8 + head + 1]
        other_total = turned[drows : 2 * drows, 8 + heads + head : 8 + heads + head + 1]
        peak = jnp.maximum(own_top, other_top)
        mine = jnp.exp2((own_top - peak) * STEEP)
        theirs = jnp.exp2((other_top - peak) * STEEP)
        whole = mine * dmix[0:drows, span] + theirs * zback[:, span].astype(jnp.float32)
        dec_ref[:, span] = (whole / (mine * own_total + theirs * other_total)).astype(jnp.bfloat16)

    for copy in started:
        copy.wait_send()
    for which in range(6):

        def drain_one(offset, carry):
            slab_copy(which, offset).wait_send()
            return carry

        lax.fori_loop(1, group, drain_one, 0)


def attention(query, key, value, dec_query, cross_key, cross_value):
    group = lax.axis_size("tp")
    tokens, dtokens = query.shape[0], dec_query.shape[0]
    rows, drows, columns = group * tokens, group * dtokens, query.shape[1] // group
    heads = columns // HEAD_DIM
    bf16, f32 = jnp.bfloat16, jnp.float32
    vmem = pl.BlockSpec(memory_space=pltpu.VMEM)
    eight = pltpu.SemaphoreType.DMA((RING,))
    return pl.pallas_call(
        kernel,
        out_shape=(
            jax.ShapeDtypeStruct((rows, columns), bf16),
            jax.ShapeDtypeStruct((drows, columns), bf16),
        ),
        in_specs=[pl.BlockSpec(memory_space=pl.ANY)] * 6,
        out_specs=(vmem, vmem),
        scratch_shapes=[
            pltpu.VMEM((group, tokens, columns), bf16),
            pltpu.VMEM((group, tokens, columns), bf16),
            pltpu.VMEM((group, tokens, columns), bf16),
            pltpu.VMEM((group, dtokens, columns), bf16),
            pltpu.VMEM((group, tokens, columns), bf16),
            pltpu.VMEM((group, tokens, columns), bf16),
            pltpu.VMEM((drows, columns), bf16),
            pltpu.VMEM((2, rows, columns), bf16),
            pltpu.VMEM((RING, 2, rows, columns), bf16),
            pltpu.VMEM((RING, 2, rows, columns), bf16),
            pltpu.VMEM((RING, 2, drows, columns), bf16),
            pltpu.VMEM((2, rows, columns), bf16),
            pltpu.VMEM((2, rows, columns), bf16),
            pltpu.VMEM((heads, 2 * rows, 1), f32),
            pltpu.VMEM((heads, 2 * rows, 1), f32),
            pltpu.VMEM((heads, 2 * rows, HEAD_DIM), f32),
            pltpu.VMEM((256, 128), f32),
            pltpu.VMEM((RING, 128, 128), f32),
            pltpu.VMEM((rows, columns), bf16),
            pltpu.VMEM((2, 8, 128), f32),
            pltpu.VMEM((rows, columns), bf16),
            pltpu.VMEM((2, 8, 128), f32),
            pltpu.VMEM((RING, 2 * drows, columns), bf16),
            pltpu.VMEM((RING, 8, 128), f32),
            pltpu.VMEM((RING, 2 * drows, columns), bf16),
            pltpu.VMEM((RING, 8, 128), f32),
            pltpu.VMEM((128, 128), f32),
            pltpu.VMEM((drows, columns), bf16),
            pltpu.VMEM((8, 128), f32),
            pltpu.VMEM((drows, columns), bf16),
            pltpu.VMEM((8, 128), f32),
            pltpu.VMEM((2 * drows, columns), f32),
        ]
        + [eight] * 16
        + [pltpu.SemaphoreType.DMA((6, group))] * 2
        + [pltpu.SemaphoreType.DMA((6,))],
        compiler_params=pltpu.CompilerParams(
            collective_id=0, has_side_effects=True, vmem_limit_bytes=67043328
        ),
    )(query, key, value, dec_query, cross_key, cross_value)


def shards(enc_query, enc_key, enc_value, dec_query, cross_key, cross_value):
    return attention(enc_query, enc_key, enc_value, dec_query, cross_key, cross_value)


def solution(mesh):
    in_specs = (P(("ctx", "tp"), None),) * 6
    out_specs = (P("ctx", "tp"), P("ctx", "tp"))
    return jax.shard_map(shards, mesh=mesh, in_specs=in_specs, out_specs=out_specs, check_vma=False)
```

```python
import functools

import jax
import jax.numpy as jnp
from jax import lax
from jax.experimental import pallas as pl
from jax.experimental.pallas import tpu as pltpu
from jax.sharding import PartitionSpec as P

HEAD_DIM = 128
RING = 8
LOG2E = 1.4426950408889634
STEEP = HEAD_DIM ** (-0.5) * LOG2E
MESH = pl.DeviceIdType.MESH
KEY_RIGHT = (1, 2, 3, 4)
VALUE_RIGHT = (1, 2, 3)


def scores_of(query, key):
    return lax.dot_general(query, key, (((1,), (1,)), ((), ())), preferred_element_type=jnp.float32)


def kernel(
    q_arg, k_arg, v_arg, dq_arg, ck_arg, cv_arg, enc_ref, dec_ref,
    q_parts, k_parts, v_parts, dq_parts, ck_parts, cv_parts,
    dq_ref, qb, kb, vb, db, ckb, cvb, top, total, acc, estat, dstat,
    esend, esend_stat, eback, eback_stat, psend, psend_stat, pback, pback_stat,
    wide, zsend, zsend_stat, zback, zback_stat, dmix,
    ks, kr, vs, vr, ds, dr, kps, kpr, vps, vpr, rs, rr, rts, rtr, ms, mr, ts, tr, self_sems,
):
    rows, columns = enc_ref.shape
    drows = dq_ref.shape[0]
    tokens = q_arg.shape[0]
    dtokens = dq_arg.shape[0]
    group = q_parts.shape[0]
    here = lax.axis_index("tp")
    heads = columns // HEAD_DIM
    me = lax.axis_index("ctx")
    plane, y, core = me // (2 * RING), (me // 2) % RING, me % 2

    def along(offset):
        return {"ctx": plane * (2 * RING) + lax.rem(y + offset + RING, RING) * 2 + core}

    twin = {"ctx": plane * (2 * RING) + y * 2 + (1 - core)}
    mirror = {"ctx": (1 - plane) * (2 * RING) + y * 2 + core}

    barrier = pltpu.get_barrier_semaphore()
    for peer in [along(offset) for offset in range(1, RING)] + [twin, mirror]:
        pl.semaphore_signal(barrier, inc=1, device_id=peer, device_id_type=MESH)
    for offset in range(1, group):
        pl.semaphore_signal(
            barrier, inc=1, device_id={"tp": lax.rem(here + offset, group)}, device_id_type=MESH
        )
    pl.semaphore_wait(barrier, RING + group)

    started = []

    def send(source, target, send_sem, recv_sem, device):
        copy = pltpu.make_async_remote_copy(
            src_ref=source, dst_ref=target, send_sem=send_sem, recv_sem=recv_sem,
            device_id=device, device_id_type=MESH,
        )
        copy.start()
        started.append(copy)

    def arrived(target, recv_sem):
        pltpu.make_async_remote_copy(
            src_ref=target, dst_ref=target, send_sem=recv_sem, recv_sem=recv_sem,
            device_id=twin, device_id_type=MESH,
        ).wait_recv()

    def onward(source, slot, buffer, send_sems, recv_sems, right):
        after, before = (slot + 1) % RING, (slot - 1) % RING
        if after in right:
            send(source, buffer(after), send_sems.at[after], recv_sems.at[after], along(1))
        if before not in right and before != 0:
            send(source, buffer(before), send_sems.at[before], recv_sems.at[before], along(-1))

    def pass_on(source, slot, buffer, send_sems, recv_sems, right):
        if slot == 0:
            onward(source, 0, buffer, send_sems, recv_sems, right)
        elif slot in right:
            if slot + 1 in right:
                send(source, buffer(slot + 1), send_sems.at[slot + 1], recv_sems.at[slot + 1], along(1))
        elif slot - 1 not in right and slot - 1 != 0:
            send(source, buffer(slot - 1), send_sems.at[slot - 1], recv_sems.at[slot - 1], along(-1))

    def key_slot(slot):
        return kb.at[slot, 0]

    def value_slot(slot):
        return vb.at[slot, 0]

    def query_slot(slot):
        return db.at[slot]

    exchanges = (
        (dq_arg, dq_parts), (k_arg, k_parts), (v_arg, v_parts),
        (ck_arg, ck_parts), (cv_arg, cv_parts), (q_arg, q_parts),
    )

    def slab(which, peer):
        argument, parts = exchanges[which]
        return argument.at[:, pl.ds(pl.multiple_of(peer * columns, 128), columns)]

    def slab_copy(which, offset):
        peer = lax.rem(here + offset, group)
        return pltpu.make_async_remote_copy(
            src_ref=slab(which, peer), dst_ref=exchanges[which][1].at[here],
            send_sem=ts.at[which, offset], recv_sem=tr.at[which, here],
            device_id={"tp": peer}, device_id_type=MESH,
        )

    def self_copy(which):
        return pltpu.make_async_copy(slab(which, here), exchanges[which][1].at[here], self_sems.at[which])

    for which in range(6):
        self_copy(which).start()

        def start_one(offset, carry):
            slab_copy(which, offset).start()
            return carry

        lax.fori_loop(1, group, start_one, 0)

    def gather(which):
        parts = exchanges[which][1]

        def wait_one(offset, carry):
            origin = lax.rem(here + offset, group)
            pltpu.make_async_remote_copy(
                src_ref=parts.at[origin], dst_ref=parts.at[origin],
                send_sem=ts.at[which, offset], recv_sem=tr.at[which, origin],
                device_id=twin, device_id_type=MESH,
            ).wait_recv()
            return carry

        lax.fori_loop(1, group, wait_one, 0)
        self_copy(which).wait()
        return parts

    estat[...] = jnp.zeros_like(estat)
    dstat[...] = jnp.zeros_like(dstat)
    wide[...] = jnp.zeros_like(wide)

    def attend(span, slots, first=False):
        count = span.stop - span.start

        def body(head, carry):
            at = pl.ds(pl.multiple_of(head * HEAD_DIM, HEAD_DIM), HEAD_DIM)
            query = qb[:, :, at].reshape(2 * rows, HEAD_DIM)[span]
            parts = [scores_of(query, kb[slot, :, :, at].reshape(2 * rows, HEAD_DIM)) for slot in slots]
            new_top = functools.reduce(jnp.maximum, [jnp.max(part, axis=1, keepdims=True) for part in parts])
            if not first:
                new_top = jnp.maximum(new_top, top[head, span])
            mixed, summed = None, None
            for slot, part in zip(slots, parts):
                weights = jnp.exp2((part - new_top) * STEEP)
                one = jnp.sum(weights, axis=1, keepdims=True)
                two = jnp.dot(
                    weights.astype(jnp.bfloat16),
                    vb[slot, :, :, at].reshape(2 * rows, HEAD_DIM),
                    preferred_element_type=jnp.float32,
                )
                summed = one if summed is None else summed + one
                mixed = two if mixed is None else mixed + two
            if not first:
                shrink = jnp.exp2((top[head, span] - new_top) * STEEP)
                summed = summed + total[head, span] * shrink
                mixed = mixed + acc[head, span] * shrink
            top[head, span] = new_top
            total[head, span] = summed
            acc[head, span] = mixed
            return carry

        lax.fori_loop(0, heads, body, 0)

    own_rows, mirror_rows, both = slice(0, rows), slice(rows, 2 * rows), slice(0, 2 * rows)

    def visit_all():
        some = RING // 2

        def body(item, carry):
            start, head = (item // heads) * some, item % heads
            at = pl.ds(pl.multiple_of(head * HEAD_DIM, HEAD_DIM), HEAD_DIM)
            query = db[pl.ds(start, some), :, :, at].reshape(some * 2 * drows, HEAD_DIM)
            part = scores_of(query, ckb[:, :, at].reshape(2 * rows, HEAD_DIM))
            row_top = jnp.max(part, axis=1, keepdims=True)
            weights = jnp.exp2((part - row_top) * STEEP)
            summed = jnp.sum(weights, axis=1, keepdims=True)
            mixed = jnp.dot(
                weights.astype(jnp.bfloat16), cvb[:, :, at].reshape(2 * rows, HEAD_DIM),
                preferred_element_type=jnp.float32,
            )
            psend[pl.ds(start, some), :, at] = mixed.astype(jnp.bfloat16).reshape(some, 2 * drows, HEAD_DIM)
            lane = lax.broadcasted_iota(jnp.int32, (some, 2 * drows, HEAD_DIM), 2)
            held = dstat[pl.ds(start, some), 0 : 2 * drows, :]
            held = jnp.where(lane == head, row_top.reshape(some, 2 * drows, 1), held)
            held = jnp.where(lane == heads + head, summed.reshape(some, 2 * drows, 1), held)
            dstat[pl.ds(start, some), 0 : 2 * drows, :] = held
            return carry

        lax.fori_loop(0, 2 * heads, body, 0)
        for slot in (4, 3, 5, 2, 6, 1, 7):
            psend_stat[slot] = jnp.transpose(dstat[slot])[0:8]
            send(psend.at[slot], pback.at[slot], rs.at[slot], rr.at[slot], along(-slot))
            send(psend_stat.at[slot], pback_stat.at[slot], rts.at[slot], rtr.at[slot], along(-slot))
        pback[0] = psend[0]
        pback_stat[0] = jnp.transpose(dstat[0])[0:8]

    def place(which, *targets):
        parts = gather(which)
        count = parts.shape[1]
        for source in range(group):
            for target in targets:
                target[source * count : (source + 1) * count, :] = parts[source]

    def hop(step):
        pair = (step,) if step == RING - step else (step, RING - step)
        for slot in pair:
            arrived(kb.at[slot, 0], kr.at[slot])
            pass_on(kb.at[slot, 0], slot, key_slot, ks, kr, KEY_RIGHT)
            send(kb.at[slot, 0], kb.at[slot, 1], kps.at[slot], kpr.at[slot], twin)
        for slot in pair:
            arrived(vb.at[slot, 0], vr.at[slot])
            pass_on(vb.at[slot, 0], slot, value_slot, vs, vr, VALUE_RIGHT)
            send(vb.at[slot, 0], vb.at[slot, 1], vps.at[slot], vpr.at[slot], twin)

    def query_hop(step):
        for slot in (step,) if step == RING - step else (step, RING - step):
            arrived(db.at[slot], dr.at[slot])
            pass_on(db.at[slot], slot, query_slot, ds, dr, KEY_RIGHT)

    def from_twin(*slots):
        for slot in slots:
            arrived(kb.at[slot, 1], kpr.at[slot])
            arrived(vb.at[slot, 1], vpr.at[slot])

    place(0, dq_ref, db.at[0, 0])
    send(dq_ref, db.at[0, 1], ms.at[0], mr.at[0], mirror)
    place(1, kb.at[0, 0])
    pass_on(kb.at[0, 0], 0, key_slot, ks, kr, KEY_RIGHT)
    send(kb.at[0, 0], kb.at[0, 1], kps.at[0], kpr.at[0], twin)
    arrived(db.at[0, 1], mr.at[0])
    pass_on(db.at[0], 0, query_slot, ds, dr, KEY_RIGHT)
    place(2, vb.at[0, 0])
    pass_on(vb.at[0, 0], 0, value_slot, vs, vr, VALUE_RIGHT)
    send(vb.at[0, 0], vb.at[0, 1], vps.at[0], vpr.at[0], twin)
    query_hop(1)
    hop(1)
    query_hop(2)
    place(3, ckb.at[0])
    send(ckb.at[0], ckb.at[1], ms.at[2], mr.at[2], twin)
    place(4, cvb.at[0])
    send(cvb.at[0], cvb.at[1], ms.at[3], mr.at[3], twin)
    hop(2)
    query_hop(3)
    place(5, qb.at[0])
    send(qb.at[0], qb.at[1], ms.at[1], mr.at[1], mirror)
    query_hop(4)
    arrived(ckb.at[1], mr.at[2])
    arrived(cvb.at[1], mr.at[3])
    visit_all()
    hop(3)
    arrived(qb.at[1], mr.at[1])
    from_twin(0)
    attend(both, (0,), True)
    from_twin(1, 7)
    attend(both, (1, 7))
    from_twin(2, 6)
    attend(both, (2, 6))
    from_twin(3, 5)
    attend(both, (3, 5))
    hop(4)
    from_twin(4)
    attend(mirror_rows, (4,))

    lane = lax.broadcasted_iota(jnp.int32, (rows, HEAD_DIM), 1)
    held = jnp.zeros((rows, HEAD_DIM), jnp.float32)
    for head in range(heads):
        esend[:, head * HEAD_DIM : (head + 1) * HEAD_DIM] = acc[head, mirror_rows].astype(jnp.bfloat16)
        held = jnp.where(lane == head, top[head, mirror_rows], held)
        held = jnp.where(lane == heads + head, total[head, mirror_rows], held)
    estat[0:rows, :] = held
    for chunk in range(2):
        esend_stat[chunk] = jnp.transpose(estat[chunk * 128 : (chunk + 1) * 128, :])[0:8]
    send(esend, eback, ms.at[4], mr.at[4], mirror)
    send(esend_stat, eback_stat, ms.at[5], mr.at[5], mirror)
    attend(own_rows, (4,))

    for slot in range(1, RING):
        arrived(pback.at[slot], rr.at[slot])
        arrived(pback_stat.at[slot], rtr.at[slot])
    stats = [pback_stat[slot] for slot in range(RING)]
    best = functools.reduce(jnp.maximum, [stat[0:heads] for stat in stats])
    joined = None
    for slot in range(RING):
        weight = jnp.exp2((stats[slot][0:heads] - best) * STEEP)
        wide[slot * 8 : slot * 8 + heads, :] = weight
        term = weight * stats[slot][heads : 2 * heads]
        joined = term if joined is None else joined + term
    zsend_stat[...] = jnp.zeros_like(zsend_stat)
    zsend_stat[0:heads, :] = best
    zsend_stat[heads : 2 * heads, :] = joined
    turned = jnp.transpose(wide[...])
    for head in range(heads):
        span = slice(head * HEAD_DIM, (head + 1) * HEAD_DIM)
        mixed = None
        for slot in range(RING):
            term = pback[slot, :, span].astype(jnp.float32) * turned[0 : 2 * drows, slot * 8 + head : slot * 8 + head + 1]
            mixed = term if mixed is None else mixed + term
        dmix[:, span] = mixed
        zsend[:, span] = mixed[drows:].astype(jnp.bfloat16)
    send(zsend, zback, ms.at[6], mr.at[6], mirror)
    send(zsend_stat, zback_stat, ms.at[7], mr.at[7], mirror)

    arrived(eback, mr.at[4])
    arrived(eback_stat, mr.at[5])
    wide[8:, :] = jnp.zeros((120, 128), jnp.float32)
    for chunk in range(2):
        wide[0:8, :] = eback_stat[chunk]
        estat[chunk * 128 : (chunk + 1) * 128, :] = jnp.transpose(wide[...])
    for head in range(heads):
        span = slice(head * HEAD_DIM, (head + 1) * HEAD_DIM)
        other_top = estat[0:rows, head : head + 1]
        other_total = estat[0:rows, heads + head : heads + head + 1]
        peak = jnp.maximum(top[head, own_rows], other_top)
        mine = jnp.exp2((top[head, own_rows] - peak) * STEEP)
        theirs = jnp.exp2((other_top - peak) * STEEP)
        whole = mine * acc[head, own_rows] + theirs * eback[:, span].astype(jnp.float32)
        enc_ref[:, span] = (whole / (mine * total[head, own_rows] + theirs * other_total)).astype(jnp.bfloat16)

    arrived(zback, mr.at[6])
    arrived(zback_stat, mr.at[7])
    wide[0:8, :] = zsend_stat[...]
    wide[8:16, :] = zback_stat[...]
    turned = jnp.transpose(wide[...])
    for head in range(heads):
        span = slice(head * HEAD_DIM, (head + 1) * HEAD_DIM)
        own_top = turned[0:drows, head : head + 1]
        own_total = turned[0:drows, heads + head : heads + head + 1]
        other_top = turned[drows : 2 * drows, 8 + head : 8 + head + 1]
        other_total = turned[drows : 2 * drows, 8 + heads + head : 8 + heads + head + 1]
        peak = jnp.maximum(own_top, other_top)
        mine = jnp.exp2((own_top - peak) * STEEP)
        theirs = jnp.exp2((other_top - peak) * STEEP)
        whole = mine * dmix[0:drows, span] + theirs * zback[:, span].astype(jnp.float32)
        dec_ref[:, span] = (whole / (mine * own_total + theirs * other_total)).astype(jnp.bfloat16)

    for copy in started:
        copy.wait_send()
    for which in range(6):

        def drain_one(offset, carry):
            slab_copy(which, offset).wait_send()
            return carry

        lax.fori_loop(1, group, drain_one, 0)


def attention(query, key, value, dec_query, cross_key, cross_value):
    group = lax.axis_size("tp")
    tokens, dtokens = query.shape[0], dec_query.shape[0]
    rows, drows, columns = group * tokens, group * dtokens, query.shape[1] // group
    heads = columns // HEAD_DIM
    bf16, f32 = jnp.bfloat16, jnp.float32
    vmem = pl.BlockSpec(memory_space=pltpu.VMEM)
    eight = pltpu.SemaphoreType.DMA((RING,))
    return pl.pallas_call(
        kernel,
        out_shape=(
            jax.ShapeDtypeStruct((rows, columns), bf16),
            jax.ShapeDtypeStruct((drows, columns), bf16),
        ),
        in_specs=[pl.BlockSpec(memory_space=pl.ANY)] * 6,
        out_specs=(vmem, vmem),
        scratch_shapes=[
            pltpu.VMEM((group, tokens, columns), bf16),
            pltpu.VMEM((group, tokens, columns), bf16),
            pltpu.VMEM((group, tokens, columns), bf16),
            pltpu.VMEM((group, dtokens, columns), bf16),
            pltpu.VMEM((group, tokens, columns), bf16),
            pltpu.VMEM((group, tokens, columns), bf16),
            pltpu.VMEM((drows, columns), bf16),
            pltpu.VMEM((2, rows, columns), bf16),
            pltpu.VMEM((RING, 2, rows, columns), bf16),
            pltpu.VMEM((RING, 2, rows, columns), bf16),
            pltpu.VMEM((RING, 2, drows, columns), bf16),
            pltpu.VMEM((2, rows, columns), bf16),
            pltpu.VMEM((2, rows, columns), bf16),
            pltpu.VMEM((heads, 2 * rows, 1), f32),
            pltpu.VMEM((heads, 2 * rows, 1), f32),
            pltpu.VMEM((heads, 2 * rows, HEAD_DIM), f32),
            pltpu.VMEM((256, 128), f32),
            pltpu.VMEM((RING, 128, 128), f32),
            pltpu.VMEM((rows, columns), bf16),
            pltpu.VMEM((2, 8, 128), f32),
            pltpu.VMEM((rows, columns), bf16),
            pltpu.VMEM((2, 8, 128), f32),
            pltpu.VMEM((RING, 2 * drows, columns), bf16),
            pltpu.VMEM((RING, 8, 128), f32),
            pltpu.VMEM((RING, 2 * drows, columns), bf16),
            pltpu.VMEM((RING, 8, 128), f32),
            pltpu.VMEM((128, 128), f32),
            pltpu.VMEM((drows, columns), bf16),
            pltpu.VMEM((8, 128), f32),
            pltpu.VMEM((drows, columns), bf16),
            pltpu.VMEM((8, 128), f32),
            pltpu.VMEM((2 * drows, columns), f32),
        ]
        + [eight] * 16
        + [pltpu.SemaphoreType.DMA((6, group))] * 2
        + [pltpu.SemaphoreType.DMA((6,))],
        compiler_params=pltpu.CompilerParams(
            collective_id=0, has_side_effects=True, vmem_limit_bytes=67043328
        ),
    )(query, key, value, dec_query, cross_key, cross_value)


def shards(enc_query, enc_key, enc_value, dec_query, cross_key, cross_value):
    return attention(enc_query, enc_key, enc_value, dec_query, cross_key, cross_value)


def solution(mesh):
    in_specs = (P(("ctx", "tp"), None),) * 6
    out_specs = (P("ctx", "tp"), P("ctx", "tp"))
    return jax.shard_map(shards, mesh=mesh, in_specs=in_specs, out_specs=out_specs, check_vma=False)
```

```python
import functools

import jax
import jax.numpy as jnp
from jax import lax
from jax.experimental import pallas as pl
from jax.experimental.pallas import tpu as pltpu
from jax.sharding import PartitionSpec as P

HEAD_DIM = 128
RING = 8
LOG2E = 1.4426950408889634
STEEP = HEAD_DIM ** (-0.5) * LOG2E
MESH = pl.DeviceIdType.MESH
KEY_RIGHT = (1, 2, 3, 4)
VALUE_RIGHT = (1, 2, 3)


def scores_of(query, key):
    return lax.dot_general(query, key, (((1,), (1,)), ((), ())), preferred_element_type=jnp.float32)


def kernel(
    q_arg, k_arg, v_arg, dq_arg, ck_arg, cv_arg, enc_ref, dec_ref,
    q_parts, k_parts, v_parts, dq_parts, ck_parts, cv_parts,
    dq_ref, qb, kb, vb, db, ckb, cvb, top, total, acc, estat, dstat,
    esend, esend_stat, eback, eback_stat, psend, psend_stat, pback, pback_stat,
    wide, zsend, zsend_stat, zback, zback_stat, dmix,
    ks, kr, vs, vr, ds, dr, kps, kpr, vps, vpr, rs, rr, rts, rtr, ms, mr, ts, tr, self_sems,
):
    rows, columns = enc_ref.shape
    drows = dq_ref.shape[0]
    tokens = q_arg.shape[0]
    dtokens = dq_arg.shape[0]
    group = q_parts.shape[0]
    here = lax.axis_index("tp")
    heads = columns // HEAD_DIM
    me = lax.axis_index("ctx")
    plane, y, core = me // (2 * RING), (me // 2) % RING, me % 2

    def along(offset):
        return {"ctx": plane * (2 * RING) + lax.rem(y + offset + RING, RING) * 2 + core}

    twin = {"ctx": plane * (2 * RING) + y * 2 + (1 - core)}
    mirror = {"ctx": (1 - plane) * (2 * RING) + y * 2 + core}

    barrier = pltpu.get_barrier_semaphore()
    for peer in [along(offset) for offset in range(1, RING)] + [twin, mirror]:
        pl.semaphore_signal(barrier, inc=1, device_id=peer, device_id_type=MESH)
    for offset in range(1, group):
        pl.semaphore_signal(
            barrier, inc=1, device_id={"tp": lax.rem(here + offset, group)}, device_id_type=MESH
        )
    pl.semaphore_wait(barrier, RING + group)

    started = []

    def send(source, target, send_sem, recv_sem, device):
        copy = pltpu.make_async_remote_copy(
            src_ref=source, dst_ref=target, send_sem=send_sem, recv_sem=recv_sem,
            device_id=device, device_id_type=MESH,
        )
        copy.start()
        started.append(copy)

    def arrived(target, recv_sem):
        pltpu.make_async_remote_copy(
            src_ref=target, dst_ref=target, send_sem=recv_sem, recv_sem=recv_sem,
            device_id=twin, device_id_type=MESH,
        ).wait_recv()

    def onward(source, slot, buffer, send_sems, recv_sems, right):
        after, before = (slot + 1) % RING, (slot - 1) % RING
        if after in right:
            send(source, buffer(after), send_sems.at[after], recv_sems.at[after], along(1))
        if before not in right and before != 0:
            send(source, buffer(before), send_sems.at[before], recv_sems.at[before], along(-1))

    def pass_on(source, slot, buffer, send_sems, recv_sems, right):
        if slot == 0:
            onward(source, 0, buffer, send_sems, recv_sems, right)
        elif slot in right:
            if slot + 1 in right:
                send(source, buffer(slot + 1), send_sems.at[slot + 1], recv_sems.at[slot + 1], along(1))
        elif slot - 1 not in right and slot - 1 != 0:
            send(source, buffer(slot - 1), send_sems.at[slot - 1], recv_sems.at[slot - 1], along(-1))

    def key_slot(slot):
        return kb.at[slot, 0]

    def value_slot(slot):
        return vb.at[slot, 0]

    def query_slot(slot):
        return db.at[slot]

    exchanges = (
        (dq_arg, dq_parts), (k_arg, k_parts), (v_arg, v_parts),
        (q_arg, q_parts), (ck_arg, ck_parts), (cv_arg, cv_parts),
    )

    def slab(which, peer):
        argument, parts = exchanges[which]
        return argument.at[:, pl.ds(pl.multiple_of(peer * columns, 128), columns)]

    def slab_copy(which, offset):
        peer = lax.rem(here + offset, group)
        return pltpu.make_async_remote_copy(
            src_ref=slab(which, peer), dst_ref=exchanges[which][1].at[here],
            send_sem=ts.at[which, offset], recv_sem=tr.at[which, here],
            device_id={"tp": peer}, device_id_type=MESH,
        )

    def self_copy(which):
        return pltpu.make_async_copy(slab(which, here), exchanges[which][1].at[here], self_sems.at[which])

    for which in range(6):
        self_copy(which).start()

        def start_one(offset, carry):
            slab_copy(which, offset).start()
            return carry

        lax.fori_loop(1, group, start_one, 0)

    def gather(which):
        parts = exchanges[which][1]

        def wait_one(offset, carry):
            origin = lax.rem(here + offset, group)
            pltpu.make_async_remote_copy(
                src_ref=parts.at[origin], dst_ref=parts.at[origin],
                send_sem=ts.at[which, offset], recv_sem=tr.at[which, origin],
                device_id=twin, device_id_type=MESH,
            ).wait_recv()
            return carry

        lax.fori_loop(1, group, wait_one, 0)
        self_copy(which).wait()
        return parts

    estat[...] = jnp.zeros_like(estat)
    dstat[...] = jnp.zeros_like(dstat)
    wide[...] = jnp.zeros_like(wide)

    def attend(span, slots, first=False):
        count = span.stop - span.start

        def body(head, carry):
            at = pl.ds(pl.multiple_of(head * HEAD_DIM, HEAD_DIM), HEAD_DIM)
            query = qb[:, :, at].reshape(2 * rows, HEAD_DIM)[span]
            parts = [scores_of(query, kb[slot, :, :, at].reshape(2 * rows, HEAD_DIM)) for slot in slots]
            new_top = functools.reduce(jnp.maximum, [jnp.max(part, axis=1, keepdims=True) for part in parts])
            if not first:
                new_top = jnp.maximum(new_top, top[head, span])
            mixed, summed = None, None
            for slot, part in zip(slots, parts):
                weights = jnp.exp2((part - new_top) * STEEP)
                one = jnp.sum(weights, axis=1, keepdims=True)
                two = jnp.dot(
                    weights.astype(jnp.bfloat16),
                    vb[slot, :, :, at].reshape(2 * rows, HEAD_DIM),
                    preferred_element_type=jnp.float32,
                )
                summed = one if summed is None else summed + one
                mixed = two if mixed is None else mixed + two
            if not first:
                shrink = jnp.exp2((top[head, span] - new_top) * STEEP)
                summed = summed + total[head, span] * shrink
                mixed = mixed + acc[head, span] * shrink
            top[head, span] = new_top
            total[head, span] = summed
            acc[head, span] = mixed
            return carry

        lax.fori_loop(0, heads, body, 0)

    own_rows, mirror_rows, both = slice(0, rows), slice(rows, 2 * rows), slice(0, 2 * rows)

    def visit_all():
        some = RING // 2

        def body(item, carry):
            start, head = (item // heads) * some, item % heads
            at = pl.ds(pl.multiple_of(head * HEAD_DIM, HEAD_DIM), HEAD_DIM)
            query = db[pl.ds(start, some), :, :, at].reshape(some * 2 * drows, HEAD_DIM)
            part = scores_of(query, ckb[:, :, at].reshape(2 * rows, HEAD_DIM))
            row_top = jnp.max(part, axis=1, keepdims=True)
            weights = jnp.exp2((part - row_top) * STEEP)
            summed = jnp.sum(weights, axis=1, keepdims=True)
            mixed = jnp.dot(
                weights.astype(jnp.bfloat16), cvb[:, :, at].reshape(2 * rows, HEAD_DIM),
                preferred_element_type=jnp.float32,
            )
            psend[pl.ds(start, some), :, at] = mixed.astype(jnp.bfloat16).reshape(some, 2 * drows, HEAD_DIM)
            lane = lax.broadcasted_iota(jnp.int32, (some, 2 * drows, HEAD_DIM), 2)
            held = dstat[pl.ds(start, some), 0 : 2 * drows, :]
            held = jnp.where(lane == head, row_top.reshape(some, 2 * drows, 1), held)
            held = jnp.where(lane == heads + head, summed.reshape(some, 2 * drows, 1), held)
            dstat[pl.ds(start, some), 0 : 2 * drows, :] = held
            return carry

        lax.fori_loop(0, 2 * heads, body, 0)
        for slot in (4, 3, 5, 2, 6, 1, 7):
            psend_stat[slot] = jnp.transpose(dstat[slot])[0:8]
            send(psend.at[slot], pback.at[slot], rs.at[slot], rr.at[slot], along(-slot))
            send(psend_stat.at[slot], pback_stat.at[slot], rts.at[slot], rtr.at[slot], along(-slot))
        pback[0] = psend[0]
        pback_stat[0] = jnp.transpose(dstat[0])[0:8]

    def place(which, *targets):
        parts = gather(which)
        count = parts.shape[1]
        for source in range(group):
            for target in targets:
                target[source * count : (source + 1) * count, :] = parts[source]

    def hop(step):
        pair = (step,) if step == RING - step else (step, RING - step)
        for slot in pair:
            arrived(kb.at[slot, 0], kr.at[slot])
            pass_on(kb.at[slot, 0], slot, key_slot, ks, kr, KEY_RIGHT)
            send(kb.at[slot, 0], kb.at[slot, 1], kps.at[slot], kpr.at[slot], twin)
        for slot in pair:
            arrived(vb.at[slot, 0], vr.at[slot])
            pass_on(vb.at[slot, 0], slot, value_slot, vs, vr, VALUE_RIGHT)
            send(vb.at[slot, 0], vb.at[slot, 1], vps.at[slot], vpr.at[slot], twin)

    def query_hop(step):
        for slot in (step,) if step == RING - step else (step, RING - step):
            arrived(db.at[slot], dr.at[slot])
            pass_on(db.at[slot], slot, query_slot, ds, dr, KEY_RIGHT)

    def from_twin(*slots):
        for slot in slots:
            arrived(kb.at[slot, 1], kpr.at[slot])
            arrived(vb.at[slot, 1], vpr.at[slot])

    place(0, dq_ref, db.at[0, 0])
    send(dq_ref, db.at[0, 1], ms.at[0], mr.at[0], mirror)
    place(1, kb.at[0, 0])
    pass_on(kb.at[0, 0], 0, key_slot, ks, kr, KEY_RIGHT)
    send(kb.at[0, 0], kb.at[0, 1], kps.at[0], kpr.at[0], twin)
    arrived(db.at[0, 1], mr.at[0])
    pass_on(db.at[0], 0, query_slot, ds, dr, KEY_RIGHT)
    place(2, vb.at[0, 0])
    pass_on(vb.at[0, 0], 0, value_slot, vs, vr, VALUE_RIGHT)
    send(vb.at[0, 0], vb.at[0, 1], vps.at[0], vpr.at[0], twin)
    query_hop(1)
    hop(1)
    query_hop(2)
    place(3, qb.at[0])
    send(qb.at[0], qb.at[1], ms.at[1], mr.at[1], mirror)
    hop(2)
    query_hop(3)
    place(4, ckb.at[0])
    send(ckb.at[0], ckb.at[1], ms.at[2], mr.at[2], twin)
    place(5, cvb.at[0])
    send(cvb.at[0], cvb.at[1], ms.at[3], mr.at[3], twin)
    hop(3)
    query_hop(4)
    arrived(ckb.at[1], mr.at[2])
    arrived(cvb.at[1], mr.at[3])
    visit_all()
    arrived(qb.at[1], mr.at[1])
    from_twin(0)
    attend(both, (0,), True)
    from_twin(1, 7)
    attend(both, (1, 7))
    from_twin(2, 6)
    attend(both, (2, 6))
    hop(4)
    from_twin(3, 5)
    attend(both, (3, 5))

    for slot in range(1, RING):
        arrived(pback.at[slot], rr.at[slot])
        arrived(pback_stat.at[slot], rtr.at[slot])
    stats = [pback_stat[slot] for slot in range(RING)]
    best = functools.reduce(jnp.maximum, [stat[0:heads] for stat in stats])
    joined = None
    for slot in range(RING):
        weight = jnp.exp2((stats[slot][0:heads] - best) * STEEP)
        wide[slot * 8 : slot * 8 + heads, :] = weight
        term = weight * stats[slot][heads : 2 * heads]
        joined = term if joined is None else joined + term
    zsend_stat[...] = jnp.zeros_like(zsend_stat)
    zsend_stat[0:heads, :] = best
    zsend_stat[heads : 2 * heads, :] = joined
    turned = jnp.transpose(wide[...])
    for head in range(heads):
        span = slice(head * HEAD_DIM, (head + 1) * HEAD_DIM)
        mixed = None
        for slot in range(RING):
            term = pback[slot, :, span].astype(jnp.float32) * turned[0 : 2 * drows, slot * 8 + head : slot * 8 + head + 1]
            mixed = term if mixed is None else mixed + term
        dmix[:, span] = mixed
        zsend[:, span] = mixed[drows:].astype(jnp.bfloat16)
    send(zsend, zback, ms.at[6], mr.at[6], mirror)
    send(zsend_stat, zback_stat, ms.at[7], mr.at[7], mirror)

    from_twin(4)
    attend(mirror_rows, (4,))

    lane = lax.broadcasted_iota(jnp.int32, (rows, HEAD_DIM), 1)
    held = jnp.zeros((rows, HEAD_DIM), jnp.float32)
    for head in range(heads):
        esend[:, head * HEAD_DIM : (head + 1) * HEAD_DIM] = acc[head, mirror_rows].astype(jnp.bfloat16)
        held = jnp.where(lane == head, top[head, mirror_rows], held)
        held = jnp.where(lane == heads + head, total[head, mirror_rows], held)
    estat[0:rows, :] = held
    for chunk in range(2):
        esend_stat[chunk] = jnp.transpose(estat[chunk * 128 : (chunk + 1) * 128, :])[0:8]
    send(esend, eback, ms.at[4], mr.at[4], mirror)
    send(esend_stat, eback_stat, ms.at[5], mr.at[5], mirror)
    attend(own_rows, (4,))

    arrived(zback, mr.at[6])
    arrived(zback_stat, mr.at[7])
    wide[0:8, :] = zsend_stat[...]
    wide[8:16, :] = zback_stat[...]
    turned = jnp.transpose(wide[...])
    for head in range(heads):
        span = slice(head * HEAD_DIM, (head + 1) * HEAD_DIM)
        own_top = turned[0:drows, head : head + 1]
        own_total = turned[0:drows, heads + head : heads + head + 1]
        other_top = turned[drows : 2 * drows, 8 + head : 8 + head + 1]
        other_total = turned[drows : 2 * drows, 8 + heads + head : 8 + heads + head + 1]
        peak = jnp.maximum(own_top, other_top)
        mine = jnp.exp2((own_top - peak) * STEEP)
        theirs = jnp.exp2((other_top - peak) * STEEP)
        whole = mine * dmix[0:drows, span] + theirs * zback[:, span].astype(jnp.float32)
        dec_ref[:, span] = (whole / (mine * own_total + theirs * other_total)).astype(jnp.bfloat16)

    arrived(eback, mr.at[4])
    arrived(eback_stat, mr.at[5])
    wide[8:, :] = jnp.zeros((120, 128), jnp.float32)
    for chunk in range(2):
        wide[0:8, :] = eback_stat[chunk]
        estat[chunk * 128 : (chunk + 1) * 128, :] = jnp.transpose(wide[...])
    for head in range(heads):
        span = slice(head * HEAD_DIM, (head + 1) * HEAD_DIM)
        other_top = estat[0:rows, head : head + 1]
        other_total = estat[0:rows, heads + head : heads + head + 1]
        peak = jnp.maximum(top[head, own_rows], other_top)
        mine = jnp.exp2((top[head, own_rows] - peak) * STEEP)
        theirs = jnp.exp2((other_top - peak) * STEEP)
        whole = mine * acc[head, own_rows] + theirs * eback[:, span].astype(jnp.float32)
        enc_ref[:, span] = (whole / (mine * total[head, own_rows] + theirs * other_total)).astype(jnp.bfloat16)

    for copy in started:
        copy.wait_send()
    for which in range(6):

        def drain_one(offset, carry):
            slab_copy(which, offset).wait_send()
            return carry

        lax.fori_loop(1, group, drain_one, 0)


def attention(query, key, value, dec_query, cross_key, cross_value):
    group = lax.axis_size("tp")
    tokens, dtokens = query.shape[0], dec_query.shape[0]
    rows, drows, columns = group * tokens, group * dtokens, query.shape[1] // group
    heads = columns // HEAD_DIM
    bf16, f32 = jnp.bfloat16, jnp.float32
    vmem = pl.BlockSpec(memory_space=pltpu.VMEM)
    eight = pltpu.SemaphoreType.DMA((RING,))
    return pl.pallas_call(
        kernel,
        out_shape=(
            jax.ShapeDtypeStruct((rows, columns), bf16),
            jax.ShapeDtypeStruct((drows, columns), bf16),
        ),
        in_specs=[pl.BlockSpec(memory_space=pl.ANY)] * 6,
        out_specs=(vmem, vmem),
        scratch_shapes=[
            pltpu.VMEM((group, tokens, columns), bf16),
            pltpu.VMEM((group, tokens, columns), bf16),
            pltpu.VMEM((group, tokens, columns), bf16),
            pltpu.VMEM((group, dtokens, columns), bf16),
            pltpu.VMEM((group, tokens, columns), bf16),
            pltpu.VMEM((group, tokens, columns), bf16),
            pltpu.VMEM((drows, columns), bf16),
            pltpu.VMEM((2, rows, columns), bf16),
            pltpu.VMEM((RING, 2, rows, columns), bf16),
            pltpu.VMEM((RING, 2, rows, columns), bf16),
            pltpu.VMEM((RING, 2, drows, columns), bf16),
            pltpu.VMEM((2, rows, columns), bf16),
            pltpu.VMEM((2, rows, columns), bf16),
            pltpu.VMEM((heads, 2 * rows, 1), f32),
            pltpu.VMEM((heads, 2 * rows, 1), f32),
            pltpu.VMEM((heads, 2 * rows, HEAD_DIM), f32),
            pltpu.VMEM((256, 128), f32),
            pltpu.VMEM((RING, 128, 128), f32),
            pltpu.VMEM((rows, columns), bf16),
            pltpu.VMEM((2, 8, 128), f32),
            pltpu.VMEM((rows, columns), bf16),
            pltpu.VMEM((2, 8, 128), f32),
            pltpu.VMEM((RING, 2 * drows, columns), bf16),
            pltpu.VMEM((RING, 8, 128), f32),
            pltpu.VMEM((RING, 2 * drows, columns), bf16),
            pltpu.VMEM((RING, 8, 128), f32),
            pltpu.VMEM((128, 128), f32),
            pltpu.VMEM((drows, columns), bf16),
            pltpu.VMEM((8, 128), f32),
            pltpu.VMEM((drows, columns), bf16),
            pltpu.VMEM((8, 128), f32),
            pltpu.VMEM((2 * drows, columns), f32),
        ]
        + [eight] * 16
        + [pltpu.SemaphoreType.DMA((6, group))] * 2
        + [pltpu.SemaphoreType.DMA((6,))],
        compiler_params=pltpu.CompilerParams(
            collective_id=0, has_side_effects=True, vmem_limit_bytes=67043328
        ),
    )(query, key, value, dec_query, cross_key, cross_value)


def shards(enc_query, enc_key, enc_value, dec_query, cross_key, cross_value):
    return attention(enc_query, enc_key, enc_value, dec_query, cross_key, cross_value)


def solution(mesh):
    in_specs = (P(("ctx", "tp"), None),) * 6
    out_specs = (P("ctx", "tp"), P("ctx", "tp"))
    return jax.shard_map(shards, mesh=mesh, in_specs=in_specs, out_specs=out_specs, check_vma=False)
```
